32 devices in a mesh: win: 4 (over x, core), src: 8 (over z, y).
Axes of the slice: x: 2, y: 2, z: 4, core: 2. Of those that a mesh axis runs over, the one named last changes fastest.
Arguments:
- strain: bfloat16 [6144, 10240], P('win', 'src'), may hold values from -1000 to 1000
- dead_mask: int32 [4, 10240], P('win', 'src'), may hold values 0 or 1
- src_index: int32 [256], replicated, may hold values from 0 to 10239
Outputs:
- correlations: float32 [4, 256, 32, 10240], P('win', 'src')
The draws below stay inside these ranges and needn't reach their ends.
All inputs are finite; a program needn't handle non-finite values. No bound on the sum of `dead_mask` on one device may be relied on, other than what follows from the above.
Results may differ from the reference program's by a relative error of at most 0.0041.
Values may be sent and summed in bfloat16 or wider, within the bound.
No kernel may reach another device: no remote copies, remote signals or barrier semaphores. Data moves between devices by JAX's collectives and lax.ppermute only.
A program may use at most 192 MiB of HBM per device.

```python
import math
import jax
import jax.numpy as jnp
from jax import lax

SENSOR_COUNT = 10240
SOURCES = 256
LAGS = 32
HALF = 32
TW = 1536
WINDOWS = 4
TOTAL_READINGS = 6144


def draw_strain(key, part):
    root_seed, key_gain, key_env = jax.random.split(key, 3)
    sinusoid_wave = jnp.clip(jax.random.normal(root_seed, (TOTAL_READINGS, SENSOR_COUNT), jnp.float32), -6.0, 6.0)
    spread = math.log(10.0)
    sensor_amplitude_factor = jnp.exp(spread * jax.random.uniform(key_gain, (1, SENSOR_COUNT), jnp.float32))
    disturbance_amplitude_profile = jnp.exp(spread * jax.random.uniform(key_env, (TOTAL_READINGS // 16, 1, SENSOR_COUNT), jnp.float32))
    disturbance_amplitude_profile = jnp.broadcast_to(disturbance_amplitude_profile, (TOTAL_READINGS // 16, 16, SENSOR_COUNT)).reshape(TOTAL_READINGS, SENSOR_COUNT)
    return (sinusoid_wave * sensor_amplitude_factor * disturbance_amplitude_profile).astype(jnp.bfloat16)


def set_ends(drawn, own_key, smallest, high):
    longest = drawn.shape.index(max(drawn.shape))
    spots = []
    for shift in (0, 1):
        where = [jax.random.randint(jax.random.fold_in(own_key, axis), (), 0, length) for axis, length in enumerate(drawn.shape)]
        where[longest] = (where[longest] + shift) % drawn.shape[longest]
        spots.append(tuple(where))
    return drawn.at[spots[0]].set(smallest).at[spots[1]].set(high)


def setup_inputs(seed: int = 0) -> dict:
    streams_of = jax.random.split(jax.random.key(seed), 4)
    strain = draw_strain(jax.random.fold_in(streams_of[3], 71), 0)
    dead_mask = set_ends((jax.random.randint(streams_of[1], (WINDOWS, SENSOR_COUNT), 0, 10) < 9).astype(jnp.int32), jax.random.fold_in(streams_of[1], 1), 0, 1)
    src_index = set_ends(jax.random.randint(streams_of[2], (SOURCES,), 0, SENSOR_COUNT), jax.random.fold_in(streams_of[2], 1), 0, SENSOR_COUNT - 1).astype(jnp.int32)
    return dict(strain=strain, dead_mask=dead_mask, src_index=src_index)


EPSILON = 1e-05

def reference(strain, dead_mask, src_index):
    alive = jnp.repeat(dead_mask, TW, axis=0) > 0
    masked = jnp.where(alive, strain, jnp.zeros((), strain.dtype)).astype(jnp.float32)
    padded = jnp.pad(jnp.abs(masked), ((HALF, HALF), (0, 0)))
    window_sums = lax.reduce_window(padded, jnp.zeros((), jnp.float32), lax.add, (2 * HALF + 1, 1), (1, 1), 'VALID')
    flat = (masked / (window_sums / (2 * HALF + 1) + EPSILON)).astype(jnp.bfloat16)
    flat_full = jnp.pad(flat, ((0, LAGS - 1), (0, 0))).astype(jnp.float32)
    corr_scale = 1.0 / math.sqrt(TW)

    def window(index_win):
        segment = lax.dynamic_slice_in_dim(flat_full, (index_win * TW).astype(jnp.int32), TW + LAGS - 1, 0)
        source_rows = segment[:TW][:, src_index].T
        stacked = jnp.stack([jnp.dot(source_rows, segment[lag_step:lag_step + TW], precision=lax.Precision.HIGHEST) for lag_step in range(LAGS)], axis=1)
        return stacked * corr_scale
    return lax.map(window, jnp.arange(WINDOWS, dtype=jnp.int32))
```

```python
import functools
import math

import jax
import jax.numpy as jnp
from jax import lax
from jax.experimental import pallas as pl
from jax.experimental.pallas import tpu as pltpu
from jax.sharding import PartitionSpec as P

LAGS = 32
HALF = 32
EPSILON = 1e-05
TILE = 192
SPAN = 2 * HALF
CHUNK = 256
ROWS = 512
FLAT_SENT = 3


def passed_along(array, axis, by):
    devices = lax.axis_size(axis)
    pairs = [(i, i + by) for i in range(devices) if 0 <= i + by < devices]
    return lax.ppermute(array, axis, pairs)


def normalize_kernel(strain_ref, mask_ref, lead_ref, trail_ref, flat_ref, rows):
    samples = strain_ref.shape[0]
    width = strain_ref.shape[1]
    alive = jnp.broadcast_to(mask_ref[...] > 0, (samples, width))
    rows[:HALF] = lead_ref[...]
    rows[HALF : HALF + samples] = jnp.where(
        alive, strain_ref[...].astype(jnp.float32), 0.0
    ).astype(jnp.bfloat16)
    rows[HALF + samples :] = trail_ref[...]
    out_rows = flat_ref.shape[0]
    row = lax.broadcasted_iota(jnp.int32, (TILE, TILE + SPAN), 0)
    col = lax.broadcasted_iota(jnp.int32, (TILE, TILE + SPAN), 1)
    band = jnp.where((col >= row) & (col <= row + SPAN), 1.0, 0.0).astype(jnp.bfloat16)
    for start in range(0, out_rows, TILE):
        count = min(TILE, out_rows - start)
        near = rows[start : start + count + SPAN]
        sums = jnp.dot(
            band[:count, : count + SPAN], jnp.abs(near), preferred_element_type=jnp.float32
        )
        center = rows[start + HALF : start + HALF + count].astype(jnp.float32)
        flat_ref[start : start + count] = (
            center / (sums / (2 * HALF + 1) + EPSILON)
        ).astype(jnp.bfloat16)


def normalize_chunk(strain, mask, lead, trail, chunk):
    samples = strain.shape[0]
    column = lambda i: (0, chunk)
    return pl.pallas_call(
        normalize_kernel,
        out_shape=jax.ShapeDtypeStruct((samples + HALF, CHUNK), jnp.bfloat16),
        grid=(1,),
        in_specs=[
            pl.BlockSpec((samples, CHUNK), column),
            pl.BlockSpec((1, CHUNK), column),
            pl.BlockSpec((HALF, CHUNK), column),
            pl.BlockSpec((SPAN, CHUNK), column),
        ],
        out_specs=pl.BlockSpec((samples + HALF, CHUNK), lambda i: (0, 0)),
        scratch_shapes=[pltpu.VMEM((samples + HALF + SPAN, CHUNK), jnp.bfloat16)],
        cost_estimate=pl.CostEstimate(
            flops=2 * (samples + HALF) * (TILE + SPAN) * CHUNK,
            bytes_accessed=4 * samples * CHUNK,
            transcendentals=0,
        ),
        name="normalize",
    )(strain, mask, lead, trail)


def select_kernel(index_ref, *refs):
    flats, out_ref = refs[:-1], refs[-1]
    total = jnp.zeros(out_ref.shape, jnp.float32)
    for chunk, flat_ref in enumerate(flats):
        channel = lax.broadcasted_iota(jnp.int32, (index_ref.shape[0], CHUNK), 1) + chunk * CHUNK
        onehot = jnp.where(index_ref[...] == channel, 1.0, 0.0).astype(jnp.bfloat16)
        total += lax.dot_general(
            onehot, flat_ref[...], (((1,), (1,)), ((), ())), preferred_element_type=jnp.float32
        )
    out_ref[...] = total.astype(jnp.bfloat16)


def select_sources(flats, index, samples):
    sources = index.shape[0]
    return pl.pallas_call(
        select_kernel,
        out_shape=jax.ShapeDtypeStruct((sources, samples), jnp.bfloat16),
        grid=(samples // 256,),
        in_specs=[pl.BlockSpec((sources, 1), lambda i: (0, 0))]
        + [pl.BlockSpec((256, CHUNK), lambda i: (i, 0))] * len(flats),
        out_specs=pl.BlockSpec((sources, 256), lambda i: (0, i)),
        cost_estimate=pl.CostEstimate(
            flops=2 * sources * samples * CHUNK * len(flats),
            bytes_accessed=2 * samples * CHUNK * len(flats),
            transcendentals=0,
        ),
        name="select",
    )(index[:, None], *flats)


def hankel_kernel(trace_ref, out_ref):
    width = out_ref.shape[1]
    for source in range(trace_ref.shape[0]):
        spread = jnp.broadcast_to(trace_ref[source : source + 1], (LAGS, width))
        shifted = pltpu.roll(spread, 0, 1, stride=1, stride_axis=0)
        out_ref[source * LAGS : (source + 1) * LAGS] = shifted.astype(jnp.bfloat16)


def hankel(traces):
    sources, samples = traces.shape
    width = samples + 128
    padded = jnp.pad(traces.astype(jnp.float32), ((0, 0), (0, 128)))
    return pl.pallas_call(
        hankel_kernel,
        out_shape=jax.ShapeDtypeStruct((sources * LAGS, width), jnp.bfloat16),
        grid=(sources // 8,),
        in_specs=[pl.BlockSpec((8, width), lambda i: (i, 0))],
        out_specs=pl.BlockSpec((8 * LAGS, width), lambda i: (i, 0)),
        cost_estimate=pl.CostEstimate(
            flops=sources * LAGS * width, bytes_accessed=2 * sources * LAGS * width, transcendentals=0
        ),
        name="hankel",
    )(padded)


def correlate_kernel(two, aliased, scale, place_ref, *refs):
    refs = list(refs)
    hankel_ref = refs.pop(0)
    first = refs.pop(0)
    second = refs.pop(0) if two else None
    if aliased:
        refs.pop(0)
    out_ref, held = refs
    depth, width = first.shape
    samples = depth - HALF

    @pl.when(pl.program_id(0) == 0)
    def _():
        held[depth:] = jnp.zeros((held.shape[0] - depth, width), held.dtype)
        if two:

            @pl.when(place_ref[1] == 1)
            def _():
                held[:depth] = first[...]

            @pl.when(place_ref[1] != 1)
            def _():
                held[:depth] = second[...]
        else:
            held[:depth] = first[...]

    product = jnp.dot(
        hankel_ref[:, :samples], held[:samples], preferred_element_type=jnp.float32
    ) + jnp.dot(hankel_ref[:, samples:], held[samples:], preferred_element_type=jnp.float32)
    out_ref[...] = (product * scale).reshape(out_ref.shape).astype(out_ref.dtype)


def correlate(rows, operands, place, scale, out=None, channels=None):
    lanes = rows.shape[0]
    sources = lanes // LAGS
    depth, width = operands[0].shape
    group = ROWS // LAGS
    whole = channels is not None
    in_specs = [pl.BlockSpec((ROWS, rows.shape[1]), lambda i, place: (i, 0))]
    in_specs += [pl.BlockSpec((depth, width), lambda i, place: (0, 0))] * len(operands)
    arguments = [rows, *operands]
    aliases = {}
    if whole:
        out_shape = jax.ShapeDtypeStruct((1, sources, LAGS, channels), jnp.float32)
        out_spec = pl.BlockSpec((1, group, LAGS, width), lambda i, place: (0, i, 0, place[0]))
        if out is not None:
            in_specs.append(pl.BlockSpec(memory_space=pl.ANY))
            arguments.append(out)
            aliases = {len(arguments): 0}
    else:
        out_shape = jax.ShapeDtypeStruct((sources, LAGS, width), jnp.bfloat16)
        out_spec = pl.BlockSpec((group, LAGS, width), lambda i, place: (i, 0, 0))
    return pl.pallas_call(
        functools.partial(correlate_kernel, len(operands) == 2, bool(aliases), scale),
        out_shape=out_shape,
        grid_spec=pltpu.PrefetchScalarGridSpec(
            num_scalar_prefetch=1,
            grid=(lanes // ROWS,),
            in_specs=in_specs,
            out_specs=out_spec,
            scratch_shapes=[pltpu.VMEM((rows.shape[1], width), jnp.bfloat16)],
        ),
        input_output_aliases=aliases,
        cost_estimate=pl.CostEstimate(
            flops=2 * lanes * rows.shape[1] * width,
            bytes_accessed=2 * lanes * rows.shape[1] + 4 * lanes * width,
            transcendentals=0,
        ),
        name="correlate" if whole else "correlate_sent",
    )(place, *arguments)


def store_kernel(place_ref, got_ref, kept_ref, out_ref):
    out_ref[...] = got_ref[...].astype(jnp.float32)[None]


def store(got, place, out):
    sources, lags, width = got.shape
    group = ROWS // LAGS
    return pl.pallas_call(
        store_kernel,
        out_shape=jax.ShapeDtypeStruct(out.shape, out.dtype),
        grid_spec=pltpu.PrefetchScalarGridSpec(
            num_scalar_prefetch=1,
            grid=(sources // group,),
            in_specs=[
                pl.BlockSpec((group, lags, width), lambda i, place: (i, 0, 0)),
                pl.BlockSpec(memory_space=pl.ANY),
            ],
            out_specs=pl.BlockSpec((1, group, lags, width), lambda i, place: (0, i, 0, place[0])),
        ),
        input_output_aliases={2: 0},
        cost_estimate=pl.CostEstimate(
            flops=0, bytes_accessed=6 * sources * lags * width, transcendentals=0
        ),
        name="store",
    )(place, got, out)


def line_of_four(strain, dead_mask, src_index):
    samples, channels = strain.shape
    devices = lax.axis_size("src")
    line = devices // 2
    chunks = channels // CHUNK
    total = channels * devices
    own = src_index.shape[0] // devices
    scale = 1.0 / math.sqrt(samples)
    me = lax.axis_index("src")
    spot, side = me // 2, me % 2

    def along(pairs):
        return [(2 * a + s, 2 * b + s) for a, b in pairs for s in range(2)]

    outer = along([(0, 1), (1, 0), (2, 3), (3, 2)])
    inner = along([(1, 2), (2, 1)])
    outward = along([(1, 0), (2, 3)])
    across = [(i, i ^ 1) for i in range(devices)]

    def masked(rows):
        return jnp.where(dead_mask > 0, rows, jnp.zeros((), rows.dtype))

    lead = passed_along(masked(strain[samples - HALF :]), "win", 1)
    trail = passed_along(masked(strain[:SPAN]), "win", -1)
    flats = [normalize_chunk(strain, dead_mask, lead, trail, c) for c in range(chunks)]

    selected = select_sources(flats, src_index - me * channels, samples)
    grouped = selected.reshape(line, 2, own, samples)
    theirs = lax.dynamic_index_in_dim(grouped, 1 - side, 1, keepdims=False)
    mine = lax.dynamic_index_in_dim(grouped, side, 1, keepdims=False)
    mine = mine + lax.ppermute(theirs, "src", across)
    traces = lax.dynamic_index_in_dim(mine, spot, 0, keepdims=False)
    for by in range(1, line):
        there = lax.dynamic_index_in_dim(mine, (spot + by) % line, 0, keepdims=False)
        pairs = along([(i, (i + by) % line) for i in range(line)])
        traces = traces + lax.ppermute(there, "src", pairs)
    partner_traces = lax.ppermute(traces, "src", across)
    own_rows = hankel(traces)
    partner_rows = hankel(partner_traces)

    first_out = [lax.ppermute(f, "src", outer) for f in flats]
    first_in = [lax.ppermute(f, "src", inner) for f in flats]
    swapped = [lax.ppermute(f, "src", across) for f in flats[:FLAT_SENT]]
    second_out = [lax.ppermute(f, "src", outward) for f in first_in]
    second_in = [lax.ppermute(f, "src", inner) for f in first_out]
    third_out = [lax.ppermute(f, "src", outward) for f in second_in]

    at_end = ((spot == 0) | (spot == line - 1)).astype(jnp.int32)
    near = spot < 2

    def places(device):
        return [jnp.stack([device * chunks + c, at_end]).astype(jnp.int32) for c in range(chunks)]

    spots = [spot, spot ^ 1, jnp.where(near, 2, 1), jnp.where(near, 3, 0)]
    here = [places(2 * s + side) for s in spots]
    there = [places(2 * s + 1 - side) for s in spots]

    work = [(0, c, [flats[c]]) for c in range(chunks)]
    work += [(1, c, [first_out[c]]) for c in range(chunks)]
    work += [(2, c, [second_out[c], first_in[c]]) for c in range(chunks)]
    work += [(3, c, [third_out[c], second_in[c]]) for c in range(chunks)]

    out = None
    waiting = []
    for slot, c, operands in work:
        if slot or c >= FLAT_SENT:
            made = correlate(partner_rows, operands, here[slot][c], scale)
            waiting.append((lax.ppermute(made, "src", across), there[slot][c]))
        out = correlate(own_rows, operands, here[slot][c], scale, out, total)
        if slot == 0 and c < FLAT_SENT:
            out = correlate(own_rows, [swapped[c]], there[0][c], scale, out, total)
        if len(waiting) > 2:
            out = store(*waiting.pop(0), out)
    for got, place in waiting:
        out = store(got, place, out)
    return out


def gathered(strain, dead_mask, src_index):
    samples, channels = strain.shape
    devices = lax.axis_size("src")
    scale = 1.0 / math.sqrt(samples)
    masked = jnp.where(dead_mask > 0, strain, jnp.zeros((), strain.dtype))
    lead = passed_along(masked[samples - HALF :], "win", 1)
    trail = passed_along(masked[:SPAN], "win", -1)
    rows = jnp.concatenate([lead, masked, trail], axis=0).astype(jnp.float32)
    sums = lax.reduce_window(
        jnp.abs(rows), jnp.zeros((), jnp.float32), lax.add, (2 * HALF + 1, 1), (1, 1), "VALID"
    )
    center = rows[HALF : rows.shape[0] - HALF]
    flat = (center / (sums / (2 * HALF + 1) + EPSILON)).astype(jnp.bfloat16)
    offset = lax.axis_index("src") * channels
    onehot = (src_index[:, None] - offset == jnp.arange(channels, dtype=jnp.int32)[None, :]).astype(
        jnp.bfloat16
    )
    selected = lax.dot_general(
        onehot, flat[:samples], (((1,), (1,)), ((), ())), preferred_element_type=jnp.float32
    )
    traces = lax.psum_scatter(
        selected.astype(jnp.bfloat16), "src", scatter_dimension=0, tiled=True
    )
    sources = traces.shape[0]
    tail = flat.shape[0] - samples
    shifted = [jnp.pad(traces, ((0, 0), (lag, tail - lag))) for lag in range(LAGS)]
    lagged = jnp.stack(shifted, axis=1).reshape(sources * LAGS, flat.shape[0])
    everywhere = lax.all_gather(flat, "src", axis=1, tiled=True)
    joined = jnp.dot(lagged, everywhere, preferred_element_type=jnp.float32) * scale
    return joined.reshape(1, sources, LAGS, channels * devices)


def shards(strain, dead_mask, src_index):
    if lax.axis_size("src") == 8 and strain.shape[1] % CHUNK == 0:
        return line_of_four(strain, dead_mask, src_index)
    return gathered(strain, dead_mask, src_index)


def solution(mesh):
    in_specs = (P("win", "src"), P("win", "src"), P())
    out_specs = P("win", "src", None, None)
    return jax.shard_map(shards, mesh=mesh, in_specs=in_specs, out_specs=out_specs, check_vma=False)
```

```python
import functools
import math

import jax
import jax.numpy as jnp
from jax import lax
from jax.experimental import pallas as pl
from jax.experimental.pallas import tpu as pltpu
from jax.sharding import PartitionSpec as P


LAGS = 32
HALF = 32
EPSILON = 1e-05
TILE = 192
SPAN = 2 * HALF
ROWS = 512
WIDTHS = (512, 512, 256)
FLAT_SENT = 1
VMEM_BYTES = 24 << 20
LAG = (4, 4, 3, 1)


def passed_along(array, axis, by):
    devices = lax.axis_size(axis)
    pairs = [(i, i + by) for i in range(devices) if 0 <= i + by < devices]
    return lax.ppermute(array, axis, pairs)


def normalize_kernel(strain_ref, mask_ref, lead_ref, trail_ref, flat_ref, rows):
    samples = strain_ref.shape[0]
    width = strain_ref.shape[1]
    alive = jnp.broadcast_to(mask_ref[...] > 0, (samples, width))
    rows[:HALF] = lead_ref[...]
    rows[HALF : HALF + samples] = jnp.where(
        alive, strain_ref[...].astype(jnp.float32), 0.0
    ).astype(jnp.bfloat16)
    rows[HALF + samples :] = trail_ref[...]
    out_rows = flat_ref.shape[0]
    row = lax.broadcasted_iota(jnp.int32, (TILE, TILE + SPAN), 0)
    col = lax.broadcasted_iota(jnp.int32, (TILE, TILE + SPAN), 1)
    band = jnp.where((col >= row) & (col <= row + SPAN), 1.0, 0.0).astype(jnp.bfloat16)
    for start in range(0, out_rows, TILE):
        count = min(TILE, out_rows - start)
        near = rows[start : start + count + SPAN]
        sums = jnp.dot(
            band[:count, : count + SPAN], jnp.abs(near), preferred_element_type=jnp.float32
        )
        center = rows[start + HALF : start + HALF + count].astype(jnp.float32)
        flat_ref[start : start + count] = (
            center / (sums / (2 * HALF + 1) + EPSILON)
        ).astype(jnp.bfloat16)


def params():
    return pltpu.CompilerParams(vmem_limit_bytes=VMEM_BYTES)


def normalize_chunk(strain, mask, lead, trail, offset, width):
    samples = strain.shape[0]

    def block(rows):
        return pl.BlockSpec((pl.Element(rows), pl.Element(width)), lambda i: (0, offset))

    return pl.pallas_call(
        normalize_kernel,
        out_shape=jax.ShapeDtypeStruct((samples + HALF, width), jnp.bfloat16),
        grid=(1,),
        in_specs=[block(samples), block(1), block(HALF), block(SPAN)],
        out_specs=pl.BlockSpec((samples + HALF, width), lambda i: (0, 0)),
        scratch_shapes=[pltpu.VMEM((samples + HALF + SPAN, width), jnp.bfloat16)],
        compiler_params=params(),
        cost_estimate=pl.CostEstimate(
            flops=2 * (samples + HALF) * (TILE + SPAN) * width,
            bytes_accessed=4 * samples * width,
            transcendentals=0,
        ),
        name="normalize",
    )(strain, mask, lead, trail)


def select_kernel(index_ref, *refs):
    flats, out_ref = refs[:-1], refs[-1]
    total = jnp.zeros(out_ref.shape, jnp.float32)
    offset = 0
    for flat_ref in flats:
        width = flat_ref.shape[1]
        channel = lax.broadcasted_iota(jnp.int32, (index_ref.shape[0], width), 1) + offset
        onehot = jnp.where(index_ref[...] == channel, 1.0, 0.0).astype(jnp.bfloat16)
        total += lax.dot_general(
            onehot, flat_ref[...], (((1,), (1,)), ((), ())), preferred_element_type=jnp.float32
        )
        offset += width
    out_ref[...] = total.astype(jnp.bfloat16)


def select_sources(flats, index, samples):
    sources = index.shape[0]
    channels = sum(f.shape[1] for f in flats)
    return pl.pallas_call(
        select_kernel,
        out_shape=jax.ShapeDtypeStruct((sources, samples), jnp.bfloat16),
        grid=(samples // 256,),
        in_specs=[pl.BlockSpec((sources, 1), lambda i: (0, 0))]
        + [pl.BlockSpec((256, f.shape[1]), lambda i: (i, 0)) for f in flats],
        out_specs=pl.BlockSpec((sources, 256), lambda i: (0, i)),
        compiler_params=params(),
        cost_estimate=pl.CostEstimate(
            flops=2 * sources * samples * channels,
            bytes_accessed=2 * samples * channels,
            transcendentals=0,
        ),
        name="select",
    )(index[:, None], *flats)


def hankel_kernel(trace_ref, out_ref):
    width = out_ref.shape[1]
    for source in range(trace_ref.shape[0]):
        spread = jnp.broadcast_to(trace_ref[source : source + 1], (LAGS, width))
        shifted = pltpu.roll(spread, 0, 1, stride=1, stride_axis=0)
        out_ref[source * LAGS : (source + 1) * LAGS] = shifted.astype(jnp.bfloat16)


def hankel(traces):
    sources, samples = traces.shape
    width = samples + 128
    padded = jnp.pad(traces.astype(jnp.float32), ((0, 0), (0, 128)))
    return pl.pallas_call(
        hankel_kernel,
        out_shape=jax.ShapeDtypeStruct((sources * LAGS, width), jnp.bfloat16),
        grid=(sources // 8,),
        in_specs=[pl.BlockSpec((8, width), lambda i: (i, 0))],
        out_specs=pl.BlockSpec((8 * LAGS, width), lambda i: (i, 0)),
        compiler_params=params(),
        cost_estimate=pl.CostEstimate(
            flops=sources * LAGS * width, bytes_accessed=2 * sources * LAGS * width, transcendentals=0
        ),
        name="hankel",
    )(padded)


def at_end(spot):
    return (spot == 0) | (spot == 3)


def origin(slot, me):
    spot, side = me >> 1, me & 1
    near = spot < 2
    there = [
        spot,
        spot ^ 1,
        jnp.where(near, 2, 1),
        jnp.where(near, 3, 0),
    ][slot]
    return 2 * there + side


def correlate_kernel(rows, two, aliased, scale, me_ref, *refs):
    refs = list(refs)
    hankels = [refs.pop(0) for _ in range(rows)]
    first = refs.pop(0)
    second = refs.pop(0) if two else None
    if aliased:
        refs.pop(0)
    held = refs.pop()
    out_ref = refs.pop(0)
    depth, width = first.shape
    step = pl.program_id(0)
    each = hankels[0].shape[0] // ROWS

    @pl.when(step == 0)
    def _():
        held[depth:] = jnp.zeros((held.shape[0] - depth, width), held.dtype)
        if two:
            end = at_end(me_ref[0] >> 1)

            @pl.when(end)
            def _():
                held[:depth] = first[...]

            @pl.when(jnp.logical_not(end))
            def _():
                held[:depth] = second[...]
        else:
            held[:depth] = first[...]

    def product(ref, at):
        lagged = ref[pl.ds(pl.multiple_of(at * ROWS, ROWS), ROWS), :]
        return jnp.dot(lagged, held[...], preferred_element_type=jnp.float32) * scale

    if rows == 1:
        out_ref[...] = product(hankels[0], step).reshape(out_ref.shape)
        return
    sent_ref = refs.pop(0)

    @pl.when(step < each)
    def _():
        sent_ref[...] = product(hankels[1], step).reshape(sent_ref.shape).astype(sent_ref.dtype)

    @pl.when(step >= each)
    def _():
        out_ref[...] = product(hankels[0], step - each).reshape(out_ref.shape)


def correlate(hankels, operands, me, place, scale, out, channels):
    lanes, span = hankels[0].shape
    sources = lanes // LAGS
    depth, width = operands[0].shape
    group = ROWS // LAGS
    each = lanes // ROWS
    rows = len(hankels)
    skip = (rows - 1) * each
    resident = pl.BlockSpec(memory_space=pltpu.VMEM)
    in_specs = [resident] * rows
    in_specs += [pl.BlockSpec((depth, width), lambda i, me: (0, 0))] * len(operands)
    arguments = [*hankels, *operands]
    aliases = {}
    if out is not None:
        in_specs.append(pl.BlockSpec(memory_space=pl.ANY))
        arguments.append(out)
        aliases = {len(arguments): 0}
    out_shape = [jax.ShapeDtypeStruct((1, sources, LAGS, channels), jnp.float32)]
    out_specs = [
        pl.BlockSpec(
            (pl.Element(1), pl.Element(group), pl.Element(LAGS), pl.Element(width)),
            lambda i, me: (
                0,
                jnp.maximum(i - skip, 0) * group,
                0,
                pl.multiple_of(place(me[0]), 128),
            ),
        )
    ]
    if rows == 2:
        out_shape.append(jax.ShapeDtypeStruct((sources, LAGS, width), jnp.bfloat16))
        out_specs.append(
            pl.BlockSpec((group, LAGS, width), lambda i, me: (jnp.minimum(i, each - 1), 0, 0))
        )
    return pl.pallas_call(
        functools.partial(correlate_kernel, rows, len(operands) == 2, bool(aliases), scale),
        out_shape=out_shape,
        grid_spec=pltpu.PrefetchScalarGridSpec(
            num_scalar_prefetch=1,
            grid=(rows * each,),
            in_specs=in_specs,
            out_specs=out_specs,
            scratch_shapes=[pltpu.VMEM((span, width), jnp.bfloat16)],
        ),
        input_output_aliases=aliases,
        compiler_params=params(),
        cost_estimate=pl.CostEstimate(
            flops=2 * rows * lanes * span * width,
            bytes_accessed=2 * depth * width + 4 * lanes * width,
            transcendentals=0,
        ),
        name="correlate",
    )(me, *arguments)


def store_kernel(me_ref, got_ref, kept_ref, out_ref):
    out_ref[...] = got_ref[...].astype(jnp.float32)[None]


def store(got, me, place, out):
    sources, lags, width = got.shape
    group = ROWS // LAGS
    return pl.pallas_call(
        store_kernel,
        out_shape=jax.ShapeDtypeStruct(out.shape, out.dtype),
        grid_spec=pltpu.PrefetchScalarGridSpec(
            num_scalar_prefetch=1,
            grid=(sources // group,),
            in_specs=[
                pl.BlockSpec((group, lags, width), lambda i, me: (i, 0, 0)),
                pl.BlockSpec(memory_space=pl.ANY),
            ],
            out_specs=pl.BlockSpec(
                (pl.Element(1), pl.Element(group), pl.Element(lags), pl.Element(width)),
                lambda i, me: (0, i * group, 0, pl.multiple_of(place(me[0]), 128)),
            ),
        ),
        input_output_aliases={2: 0},
        compiler_params=params(),
        cost_estimate=pl.CostEstimate(
            flops=0, bytes_accessed=6 * sources * lags * width, transcendentals=0
        ),
        name="store",
    )(me, got, out)


def hop(array, pairs):
    return lax.ppermute(array, "src", pairs)


def line_of_four(strain, dead_mask, src_index):
    samples, channels = strain.shape
    devices = lax.axis_size("src")
    line = devices // 2
    count = len(WIDTHS)
    offsets = [sum(WIDTHS[:c]) for c in range(count)]
    total = channels * devices
    own = src_index.shape[0] // devices
    scale = 1.0 / math.sqrt(samples)
    me = lax.axis_index("src")
    spot, side = me >> 1, me & 1

    def along(pairs):
        return [(2 * a + s, 2 * b + s) for a, b in pairs for s in range(2)]

    outer = along([(0, 1), (1, 0), (2, 3), (3, 2)])
    inner = along([(1, 2), (2, 1)])
    outward = along([(1, 0), (2, 3)])
    across = [(i, i ^ 1) for i in range(devices)]

    def masked(rows):
        return jnp.where(dead_mask > 0, rows, jnp.zeros((), rows.dtype))

    lead = passed_along(masked(strain[samples - HALF :]), "win", 1)
    trail = passed_along(masked(strain[:SPAN]), "win", -1)
    flats = []
    for c in range(count):
        flats.append(
            normalize_chunk(strain, dead_mask, lead, trail, offsets[c], WIDTHS[c])
        )

    selected = select_sources(flats, src_index - me * channels, samples)
    grouped = selected.reshape(line, 2, own, samples)
    theirs = lax.dynamic_index_in_dim(grouped, 1 - side, 1, keepdims=False)
    mine = lax.dynamic_index_in_dim(grouped, side, 1, keepdims=False)
    mine = mine + hop(theirs, across)
    traces = lax.dynamic_index_in_dim(mine, spot, 0, keepdims=False)
    for by in range(1, line):
        there = lax.dynamic_index_in_dim(mine, (spot + by) & (line - 1), 0, keepdims=False)
        traces = traces + hop(there, along([(i, (i + by) % line) for i in range(line)]))
    partner_traces = hop(traces, across)
    own_rows = hankel(traces)
    partner_rows = hankel(partner_traces)

    def hops(arrays, pairs):
        return [hop(a, pairs) for a in arrays]

    first_out = hops(flats, outer)
    first_in = hops(flats, inner)
    swapped = hops(flats[:FLAT_SENT], across)
    second_out = hops(first_in, outward)
    second_in = hops(first_out, inner)
    third_out = hops(second_in, outward)

    arrivals = [
        [[f] for f in flats],
        [[f] for f in first_out],
        [list(pair) for pair in zip(second_out, first_in)],
        [list(pair) for pair in zip(third_out, second_in)],
    ]
    here = jnp.reshape(me, (1,)).astype(jnp.int32)
    out = None
    waiting = []

    def place(slot, c, partner):
        return lambda me: (origin(slot, me) ^ partner) * channels + offsets[c]

    for slot in range(line):
        for c in range(count):
            if slot == 0 and c < FLAT_SENT:
                for partner, chunk in ((0, flats[c]), (1, swapped[c])):
                    (out,) = correlate(
                        [own_rows], [chunk], here, place(slot, c, partner), scale, out, total
                    )
                continue
            out, made = correlate(
                [own_rows, partner_rows],
                arrivals[slot][c],
                here,
                place(slot, c, 0),
                scale,
                out,
                total,
            )
            waiting.append((hop(made, across), here, place(slot, c, 1)))
            while len(waiting) > LAG[slot]:
                out = store(*waiting.pop(0), out)
    while waiting:
        out = store(*waiting.pop(0), out)
    return out


def gathered(strain, dead_mask, src_index):
    samples, channels = strain.shape
    devices = lax.axis_size("src")
    scale = 1.0 / math.sqrt(samples)
    masked = jnp.where(dead_mask > 0, strain, jnp.zeros((), strain.dtype))
    lead = passed_along(masked[samples - HALF :], "win", 1)
    trail = passed_along(masked[:SPAN], "win", -1)
    rows = jnp.concatenate([lead, masked, trail], axis=0).astype(jnp.float32)
    sums = lax.reduce_window(
        jnp.abs(rows), jnp.zeros((), jnp.float32), lax.add, (2 * HALF + 1, 1), (1, 1), "VALID"
    )
    center = rows[HALF : rows.shape[0] - HALF]
    flat = (center / (sums / (2 * HALF + 1) + EPSILON)).astype(jnp.bfloat16)
    offset = lax.axis_index("src") * channels
    onehot = (src_index[:, None] - offset == jnp.arange(channels, dtype=jnp.int32)[None, :]).astype(
        jnp.bfloat16
    )
    selected = lax.dot_general(
        onehot, flat[:samples], (((1,), (1,)), ((), ())), preferred_element_type=jnp.float32
    )
    traces = lax.psum_scatter(
        selected.astype(jnp.bfloat16), "src", scatter_dimension=0, tiled=True
    )
    sources = traces.shape[0]
    tail = flat.shape[0] - samples
    shifted = [jnp.pad(traces, ((0, 0), (lag, tail - lag))) for lag in range(LAGS)]
    lagged = jnp.stack(shifted, axis=1).reshape(sources * LAGS, flat.shape[0])
    everywhere = lax.all_gather(flat, "src", axis=1, tiled=True)
    joined = jnp.dot(lagged, everywhere, preferred_element_type=jnp.float32) * scale
    return joined.reshape(1, sources, LAGS, channels * devices)


def lined(devices, channels):
    return devices == 8 and channels == sum(WIDTHS)


def shards(strain, dead_mask, src_index):
    if lined(lax.axis_size("src"), strain.shape[1]):
        return line_of_four(strain, dead_mask, src_index)
    return gathered(strain, dead_mask, src_index)


def solution(mesh):
    in_specs = (P("win", "src"), P("win", "src"), P())
    out_specs = P("win", "src", None, None)
    return jax.shard_map(shards, mesh=mesh, in_specs=in_specs, out_specs=out_specs, check_vma=False)
```

```python
import functools
import math

import jax
import jax.numpy as jnp
from jax import lax
from jax.experimental import pallas as pl
from jax.experimental.pallas import tpu as pltpu
from jax.sharding import PartitionSpec as P


LAGS = 32
HALF = 32
EPSILON = 1e-05
TILE = 192
SPAN = 2 * HALF
ROWS = 512
VMEM_BYTES = 24 << 20

WIDTHS = (384, 512, 256, 128)
EARLY = (0, 1, 2, 3)
LATE = (1, 0, 2, 3)
STEPS = (
    [(0, c) for c in EARLY[1:]]
    + [(1, c) for c in EARLY]
    + [(2, c) for c in LATE]
    + [(3, c) for c in LATE]
)
STORED = {(1, 3): 4, (2, 1): 3, (2, 2): 1, (2, 3): 3, (3, 0): 1}


def passed_along(array, axis, by):
    devices = lax.axis_size(axis)
    pairs = [(i, i + by) for i in range(devices) if 0 <= i + by < devices]
    return lax.ppermute(array, axis, pairs)


def normalize_kernel(offset, masked_ref, lead_ref, trail_ref, flat_ref, rows):
    samples = masked_ref.shape[0]
    columns = pl.ds(offset, flat_ref.shape[1])
    pltpu.sync_copy(masked_ref.at[:, columns], rows.at[pl.ds(HALF, samples)])
    rows[:HALF] = lead_ref[...]
    rows[HALF + samples :] = trail_ref[...]
    out_rows = flat_ref.shape[0]
    row = lax.broadcasted_iota(jnp.int32, (TILE, TILE + SPAN), 0)
    col = lax.broadcasted_iota(jnp.int32, (TILE, TILE + SPAN), 1)
    band = jnp.where((col >= row) & (col <= row + SPAN), 1.0, 0.0).astype(jnp.bfloat16)
    for start in range(0, out_rows, TILE):
        count = min(TILE, out_rows - start)
        near = rows[start : start + count + SPAN]
        sums = jnp.dot(
            band[:count, : count + SPAN], jnp.abs(near), preferred_element_type=jnp.float32
        )
        center = rows[start + HALF : start + HALF + count].astype(jnp.float32)
        flat_ref[start : start + count] = (
            center / (sums / (2 * HALF + 1) + EPSILON)
        ).astype(jnp.bfloat16)


def params():
    return pltpu.CompilerParams(vmem_limit_bytes=VMEM_BYTES)


def normalize_chunk(masked, lead, trail, offset, width):
    samples = masked.shape[0]

    def block(rows):
        return pl.BlockSpec((pl.Element(rows), pl.Element(width)), lambda i: (0, offset))

    return pl.pallas_call(
        functools.partial(normalize_kernel, offset),
        out_shape=jax.ShapeDtypeStruct((samples + HALF, width), jnp.bfloat16),
        grid=(1,),
        in_specs=[pl.BlockSpec(memory_space=pltpu.HBM), block(HALF), block(SPAN)],
        out_specs=pl.BlockSpec((samples + HALF, width), lambda i: (0, 0)),
        scratch_shapes=[pltpu.VMEM((samples + HALF + SPAN, width), jnp.bfloat16)],
        compiler_params=params(),
        cost_estimate=pl.CostEstimate(
            flops=2 * (samples + HALF) * (TILE + SPAN) * width,
            bytes_accessed=4 * samples * width,
            transcendentals=0,
        ),
        name="normalize",
    )(masked, lead, trail)


def select_kernel(index_ref, *refs):
    flats, out_ref = refs[:-1], refs[-1]
    total = jnp.zeros(out_ref.shape, jnp.float32)
    offset = 0
    for flat_ref in flats:
        width = flat_ref.shape[1]
        channel = lax.broadcasted_iota(jnp.int32, (index_ref.shape[0], width), 1) + offset
        onehot = jnp.where(index_ref[...] == channel, 1.0, 0.0).astype(jnp.bfloat16)
        total += lax.dot_general(
            onehot, flat_ref[...], (((1,), (1,)), ((), ())), preferred_element_type=jnp.float32
        )
        offset += width
    out_ref[...] = total.astype(jnp.bfloat16)


def select_sources(flats, index, samples):
    sources = index.shape[0]
    channels = sum(f.shape[1] for f in flats)
    return pl.pallas_call(
        select_kernel,
        out_shape=jax.ShapeDtypeStruct((sources, samples), jnp.bfloat16),
        grid=(samples // 256,),
        in_specs=[pl.BlockSpec((sources, 1), lambda i: (0, 0))]
        + [pl.BlockSpec((256, f.shape[1]), lambda i: (i, 0)) for f in flats],
        out_specs=pl.BlockSpec((sources, 256), lambda i: (0, i)),
        compiler_params=params(),
        cost_estimate=pl.CostEstimate(
            flops=2 * sources * samples * channels,
            bytes_accessed=2 * samples * channels,
            transcendentals=0,
        ),
        name="select",
    )(index[:, None], *flats)


def hankel_kernel(trace_ref, out_ref):
    width = out_ref.shape[1]
    for source in range(trace_ref.shape[0]):
        spread = jnp.broadcast_to(trace_ref[source : source + 1], (LAGS, width))
        shifted = pltpu.roll(spread, 0, 1, stride=1, stride_axis=0)
        out_ref[source * LAGS : (source + 1) * LAGS] = shifted.astype(jnp.bfloat16)


def hankel(traces):
    sources, samples = traces.shape
    width = samples + 128
    padded = jnp.pad(traces.astype(jnp.float32), ((0, 0), (0, 128)))
    return pl.pallas_call(
        hankel_kernel,
        out_shape=jax.ShapeDtypeStruct((sources * LAGS, width), jnp.bfloat16),
        grid=(sources // 8,),
        in_specs=[pl.BlockSpec((8, width), lambda i: (i, 0))],
        out_specs=pl.BlockSpec((8 * LAGS, width), lambda i: (i, 0)),
        compiler_params=params(),
        cost_estimate=pl.CostEstimate(
            flops=sources * LAGS * width, bytes_accessed=2 * sources * LAGS * width, transcendentals=0
        ),
        name="hankel",
    )(padded)


def at_end(spot):
    return (spot == 0) | (spot == 3)


def origin(slot, me):
    spot, side = me >> 1, me & 1
    near = spot < 2
    there = [
        spot,
        spot ^ 1,
        jnp.where(near, 2, 1),
        jnp.where(near, 3, 0),
    ][slot]
    return 2 * there + side


def correlate_kernel(rows, two, aliased, scale, me_ref, *refs):
    refs = list(refs)
    hankels = [refs.pop(0) for _ in range(rows)]
    first = refs.pop(0)
    second = refs.pop(0) if two else None
    if aliased:
        refs.pop(0)
    held = refs.pop()
    out_ref = refs.pop(0)
    depth, width = first.shape
    step = pl.program_id(0)
    each = hankels[0].shape[0] // ROWS

    @pl.when(step == 0)
    def _():
        held[depth:] = jnp.zeros((held.shape[0] - depth, width), held.dtype)
        if two:
            end = at_end(me_ref[0] >> 1)

            @pl.when(end)
            def _():
                held[:depth] = first[...]

            @pl.when(jnp.logical_not(end))
            def _():
                held[:depth] = second[...]
        else:
            held[:depth] = first[...]

    def product(ref, at):
        lagged = ref[pl.ds(pl.multiple_of(at * ROWS, ROWS), ROWS), :]
        return jnp.dot(lagged, held[...], preferred_element_type=jnp.float32) * scale

    if rows == 1:
        out_ref[...] = product(hankels[0], step).reshape(out_ref.shape)
        return
    sent_ref = refs.pop(0)

    @pl.when(step < each)
    def _():
        sent_ref[...] = product(hankels[1], step).reshape(sent_ref.shape).astype(sent_ref.dtype)

    @pl.when(step >= each)
    def _():
        out_ref[...] = product(hankels[0], step - each).reshape(out_ref.shape)


def correlate(hankels, operands, me, place, scale, out, channels):
    lanes, span = hankels[0].shape
    sources = lanes // LAGS
    depth, width = operands[0].shape
    group = ROWS // LAGS
    each = lanes // ROWS
    rows = len(hankels)
    skip = (rows - 1) * each
    resident = pl.BlockSpec(memory_space=pltpu.VMEM)
    in_specs = [resident] * rows
    in_specs += [pl.BlockSpec((depth, width), lambda i, me: (0, 0))] * len(operands)
    arguments = [*hankels, *operands]
    aliases = {}
    if out is not None:
        in_specs.append(pl.BlockSpec(memory_space=pl.ANY))
        arguments.append(out)
        aliases = {len(arguments): 0}
    out_shape = [jax.ShapeDtypeStruct((1, sources, LAGS, channels), jnp.float32)]
    out_specs = [
        pl.BlockSpec(
            (pl.Element(1), pl.Element(group), pl.Element(LAGS), pl.Element(width)),
            lambda i, me: (
                0,
                jnp.maximum(i - skip, 0) * group,
                0,
                pl.multiple_of(place(me[0]), 128),
            ),
        )
    ]
    if rows == 2:
        out_shape.append(jax.ShapeDtypeStruct((sources, LAGS, width), jnp.bfloat16))
        out_specs.append(
            pl.BlockSpec((group, LAGS, width), lambda i, me: (jnp.minimum(i, each - 1), 0, 0))
        )
    return pl.pallas_call(
        functools.partial(correlate_kernel, rows, len(operands) == 2, bool(aliases), scale),
        out_shape=out_shape,
        grid_spec=pltpu.PrefetchScalarGridSpec(
            num_scalar_prefetch=1,
            grid=(rows * each,),
            in_specs=in_specs,
            out_specs=out_specs,
            scratch_shapes=[pltpu.VMEM((span, width), jnp.bfloat16)],
        ),
        input_output_aliases=aliases,
        compiler_params=params(),
        cost_estimate=pl.CostEstimate(
            flops=2 * rows * lanes * span * width,
            bytes_accessed=2 * depth * width + 4 * lanes * width,
            transcendentals=0,
        ),
        name="correlate",
    )(me, *arguments)


def store_kernel(me_ref, got_ref, kept_ref, out_ref):
    out_ref[...] = got_ref[...].astype(jnp.float32)[None]


def store(got, me, place, out):
    sources, lags, width = got.shape
    group = ROWS // LAGS
    return pl.pallas_call(
        store_kernel,
        out_shape=jax.ShapeDtypeStruct(out.shape, out.dtype),
        grid_spec=pltpu.PrefetchScalarGridSpec(
            num_scalar_prefetch=1,
            grid=(sources // group,),
            in_specs=[
                pl.BlockSpec((group, lags, width), lambda i, me: (i, 0, 0)),
                pl.BlockSpec(memory_space=pl.ANY),
            ],
            out_specs=pl.BlockSpec(
                (pl.Element(1), pl.Element(group), pl.Element(lags), pl.Element(width)),
                lambda i, me: (0, i * group, 0, pl.multiple_of(place(me[0]), 128)),
            ),
        ),
        input_output_aliases={2: 0},
        compiler_params=params(),
        cost_estimate=pl.CostEstimate(
            flops=0, bytes_accessed=6 * sources * lags * width, transcendentals=0
        ),
        name="store",
    )(me, got, out)


def hop(array, pairs):
    return lax.ppermute(array, "src", pairs)


def line_of_four(strain, dead_mask, src_index):
    samples, channels = strain.shape
    devices = lax.axis_size("src")
    line = devices // 2
    count = len(WIDTHS)
    offsets = [sum(WIDTHS[:c]) for c in range(count)]
    total = channels * devices
    own = src_index.shape[0] // devices
    scale = 1.0 / math.sqrt(samples)
    me = lax.axis_index("src")
    spot, side = me >> 1, me & 1

    def along(pairs):
        return [(2 * a + s, 2 * b + s) for a, b in pairs for s in range(2)]

    outer = along([(0, 1), (1, 0), (2, 3), (3, 2)])
    inner = along([(1, 2), (2, 1)])
    outward = along([(1, 0), (2, 3)])
    across = [(i, i ^ 1) for i in range(devices)]

    def masked(rows):
        return jnp.where(dead_mask > 0, rows, jnp.zeros((), rows.dtype))

    lead = passed_along(masked(strain[samples - HALF :]), "win", 1)
    trail = passed_along(masked(strain[:SPAN]), "win", -1)
    alive = masked(strain)
    flats = []
    for c in range(count):
        flats.append(
            normalize_chunk(alive, lead, trail, offsets[c], WIDTHS[c])
        )

    selected = select_sources(flats, src_index - me * channels, samples)
    grouped = selected.reshape(line, 2, own, samples)
    theirs = lax.dynamic_index_in_dim(grouped, 1 - side, 1, keepdims=False)
    mine = lax.dynamic_index_in_dim(grouped, side, 1, keepdims=False)
    mine = mine + hop(theirs, across)
    traces = lax.dynamic_index_in_dim(mine, spot, 0, keepdims=False)
    for by in range(1, line):
        there = lax.dynamic_index_in_dim(mine, (spot + by) & (line - 1), 0, keepdims=False)
        traces = traces + hop(there, along([(i, (i + by) % line) for i in range(line)]))
    partner_traces = hop(traces, across)
    own_rows = hankel(traces)
    partner_rows = hankel(partner_traces)

    def hops(arrays, pairs):
        return [hop(a, pairs) for a in arrays]

    first_out = hops(flats, outer)
    first_in = hops(flats, inner)
    swapped = hop(flats[0], across)
    second_out = hops(first_in, outward)
    second_in = hops(first_out, inner)
    third_out = hops(second_in, outward)

    arrivals = [
        [[f] for f in flats],
        [[f] for f in first_out],
        [list(pair) for pair in zip(second_out, first_in)],
        [list(pair) for pair in zip(third_out, second_in)],
    ]
    here = jnp.reshape(me, (1,)).astype(jnp.int32)
    out = None
    waiting = []

    def place(slot, c, partner):
        return lambda me: (origin(slot, me) ^ partner) * channels + offsets[c]

    def add(slot, c, partner, chunk, hankels):
        nonlocal out
        out, *sent = correlate(
            hankels, chunk, here, place(slot, c, partner), scale, out, total
        )
        return sent

    def keep():
        nonlocal out
        out = store(*waiting.pop(0), out)

    add(0, 0, 0, [flats[0]], [own_rows])
    for slot, c in STEPS:
        (made,) = add(slot, c, 0, arrivals[slot][c], [own_rows, partner_rows])
        waiting.append((hop(made, across), here, place(slot, c, 1)))
        if (slot, c) == (0, count - 1):
            add(0, 0, 1, [swapped], [own_rows])
        for _ in range(STORED.get((slot, c), 0)):
            keep()
    while waiting:
        keep()
    return out


def gathered(strain, dead_mask, src_index):
    samples, channels = strain.shape
    devices = lax.axis_size("src")
    scale = 1.0 / math.sqrt(samples)
    masked = jnp.where(dead_mask > 0, strain, jnp.zeros((), strain.dtype))
    lead = passed_along(masked[samples - HALF :], "win", 1)
    trail = passed_along(masked[:SPAN], "win", -1)
    rows = jnp.concatenate([lead, masked, trail], axis=0).astype(jnp.float32)
    sums = lax.reduce_window(
        jnp.abs(rows), jnp.zeros((), jnp.float32), lax.add, (2 * HALF + 1, 1), (1, 1), "VALID"
    )
    center = rows[HALF : rows.shape[0] - HALF]
    flat = (center / (sums / (2 * HALF + 1) + EPSILON)).astype(jnp.bfloat16)
    offset = lax.axis_index("src") * channels
    onehot = (src_index[:, None] - offset == jnp.arange(channels, dtype=jnp.int32)[None, :]).astype(
        jnp.bfloat16
    )
    selected = lax.dot_general(
        onehot, flat[:samples], (((1,), (1,)), ((), ())), preferred_element_type=jnp.float32
    )
    traces = lax.psum_scatter(
        selected.astype(jnp.bfloat16), "src", scatter_dimension=0, tiled=True
    )
    sources = traces.shape[0]
    tail = flat.shape[0] - samples
    shifted = [jnp.pad(traces, ((0, 0), (lag, tail - lag))) for lag in range(LAGS)]
    lagged = jnp.stack(shifted, axis=1).reshape(sources * LAGS, flat.shape[0])
    everywhere = lax.all_gather(flat, "src", axis=1, tiled=True)
    joined = jnp.dot(lagged, everywhere, preferred_element_type=jnp.float32) * scale
    return joined.reshape(1, sources, LAGS, channels * devices)


def lined(devices, channels):
    return devices == 8 and channels == sum(WIDTHS)


def shards(strain, dead_mask, src_index):
    if lined(lax.axis_size("src"), strain.shape[1]):
        return line_of_four(strain, dead_mask, src_index)
    return gathered(strain, dead_mask, src_index)


def solution(mesh):
    in_specs = (P("win", "src"), P("win", "src"), P())
    out_specs = P("win", "src", None, None)
    return jax.shard_map(shards, mesh=mesh, in_specs=in_specs, out_specs=out_specs, check_vma=False)
```

```python
import functools
import math

import jax
import jax.numpy as jnp
from jax import lax
from jax.experimental import pallas as pl
from jax.experimental.pallas import tpu as pltpu
from jax.sharding import PartitionSpec as P


LAGS = 32
HALF = 32
EPSILON = 1e-05
TILE = 192
SPAN = 2 * HALF
ROWS = 512
VMEM_BYTES = 24 << 20

WIDTHS = (384, 512, 256, 128)
EARLY = (0, 1, 2, 3)
LATE = (1, 0, 2, 3)
STEPS = (
    [(0, c) for c in EARLY[1:]]
    + [(1, c) for c in EARLY]
    + [(2, c) for c in LATE]
    + [(3, c) for c in LATE]
)
STORED = {(1, 3): 4, (2, 1): 3, (2, 2): 1, (2, 3): 3, (3, 0): 1}


def passed_along(array, axis, by):
    devices = lax.axis_size(axis)
    pairs = [(i, i + by) for i in range(devices) if 0 <= i + by < devices]
    return lax.ppermute(array, axis, pairs)


def normalize_kernel(offset, strain_ref, mask_ref, lead_ref, trail_ref, flat_ref, held, rows):
    samples = strain_ref.shape[0]
    columns = pl.ds(offset, flat_ref.shape[1])
    pltpu.sync_copy(strain_ref.at[:, columns], held)
    alive = jnp.broadcast_to(mask_ref[...] > 0, held.shape)
    rows[:HALF] = lead_ref[...]
    rows[HALF : HALF + samples] = jnp.where(
        alive, held[...].astype(jnp.float32), 0.0
    ).astype(jnp.bfloat16)
    rows[HALF + samples :] = trail_ref[...]
    out_rows = flat_ref.shape[0]
    row = lax.broadcasted_iota(jnp.int32, (TILE, TILE + SPAN), 0)
    col = lax.broadcasted_iota(jnp.int32, (TILE, TILE + SPAN), 1)
    band = jnp.where((col >= row) & (col <= row + SPAN), 1.0, 0.0).astype(jnp.bfloat16)
    for start in range(0, out_rows, TILE):
        count = min(TILE, out_rows - start)
        near = rows[start : start + count + SPAN]
        sums = jnp.dot(
            band[:count, : count + SPAN], jnp.abs(near), preferred_element_type=jnp.float32
        )
        center = rows[start + HALF : start + HALF + count].astype(jnp.float32)
        flat_ref[start : start + count] = (
            center / (sums / (2 * HALF + 1) + EPSILON)
        ).astype(jnp.bfloat16)


def params():
    return pltpu.CompilerParams(vmem_limit_bytes=VMEM_BYTES)


def normalize_chunk(strain, mask, lead, trail, offset, width):
    samples = strain.shape[0]

    def block(rows):
        return pl.BlockSpec((pl.Element(rows), pl.Element(width)), lambda i: (0, offset))

    return pl.pallas_call(
        functools.partial(normalize_kernel, offset),
        out_shape=jax.ShapeDtypeStruct((samples + HALF, width), jnp.bfloat16),
        grid=(1,),
        in_specs=[pl.BlockSpec(memory_space=pltpu.HBM), block(1), block(HALF), block(SPAN)],
        out_specs=pl.BlockSpec((samples + HALF, width), lambda i: (0, 0)),
        scratch_shapes=[
            pltpu.VMEM((samples, width), jnp.bfloat16),
            pltpu.VMEM((samples + HALF + SPAN, width), jnp.bfloat16),
        ],
        compiler_params=pltpu.CompilerParams(vmem_limit_bytes=52 << 20),
        cost_estimate=pl.CostEstimate(
            flops=2 * (samples + HALF) * (TILE + SPAN) * width,
            bytes_accessed=4 * samples * width,
            transcendentals=0,
        ),
        name="normalize",
    )(strain, mask, lead, trail)


def select_kernel(own, me_ref, index_ref, *refs):
    flats, (theirs_ref, mine_ref) = refs[:-2], refs[-2:]
    half = theirs_ref.shape[0]
    me = me_ref[0]
    spot, side = me >> 1, me & 1
    line = half // own
    index = jnp.concatenate(
        [
            index_ref[pl.ds(pl.multiple_of(block * own, own), own), :]
            for far in (1, 0)
            for block in [
                2 * ((spot + by) & (line - 1)) + (side ^ far) for by in range(line)
            ]
        ],
        axis=0,
    )
    offset = me * sum(flat.shape[1] for flat in flats)
    total = jnp.zeros((2 * half, theirs_ref.shape[1]), jnp.float32)
    for flat_ref in flats:
        width = flat_ref.shape[1]
        channel = lax.broadcasted_iota(jnp.int32, (2 * half, width), 1) + offset
        onehot = jnp.where(index == channel, 1.0, 0.0).astype(jnp.bfloat16)
        total += lax.dot_general(
            onehot, flat_ref[...], (((1,), (1,)), ((), ())), preferred_element_type=jnp.float32
        )
        offset += width
    theirs_ref[...] = total[:half].astype(jnp.bfloat16)
    mine_ref[...] = total[half:].astype(jnp.bfloat16)


def select_sources(flats, index, me, samples, own):
    sources = index.shape[0]
    channels = sum(f.shape[1] for f in flats)
    return pl.pallas_call(
        functools.partial(select_kernel, own),
        out_shape=[jax.ShapeDtypeStruct((sources // 2, samples), jnp.bfloat16)] * 2,
        grid_spec=pltpu.PrefetchScalarGridSpec(
            num_scalar_prefetch=1,
            grid=(samples // 256,),
            in_specs=[pl.BlockSpec((sources, 1), lambda i, me: (0, 0))]
            + [pl.BlockSpec((256, f.shape[1]), lambda i, me: (i, 0)) for f in flats],
            out_specs=[pl.BlockSpec((sources // 2, 256), lambda i, me: (0, i))] * 2,
        ),
        compiler_params=params(),
        cost_estimate=pl.CostEstimate(
            flops=2 * sources * samples * channels,
            bytes_accessed=2 * samples * channels,
            transcendentals=0,
        ),
        name="select",
    )(me, index[:, None], *flats)


def hankel_kernel(trace_ref, out_ref):
    width = out_ref.shape[1]
    for source in range(trace_ref.shape[0]):
        spread = jnp.broadcast_to(trace_ref[source : source + 1], (LAGS, width))
        shifted = pltpu.roll(spread, 0, 1, stride=1, stride_axis=0)
        out_ref[source * LAGS : (source + 1) * LAGS] = shifted.astype(jnp.bfloat16)


def hankel(traces):
    sources, samples = traces.shape
    width = samples + 128
    padded = jnp.pad(traces.astype(jnp.float32), ((0, 0), (0, 128)))
    return pl.pallas_call(
        hankel_kernel,
        out_shape=jax.ShapeDtypeStruct((sources * LAGS, width), jnp.bfloat16),
        grid=(sources // 8,),
        in_specs=[pl.BlockSpec((8, width), lambda i: (i, 0))],
        out_specs=pl.BlockSpec((8 * LAGS, width), lambda i: (i, 0)),
        compiler_params=params(),
        cost_estimate=pl.CostEstimate(
            flops=sources * LAGS * width, bytes_accessed=2 * sources * LAGS * width, transcendentals=0
        ),
        name="hankel",
    )(padded)


def at_end(spot):
    return (spot == 0) | (spot == 3)


def origin(slot, me):
    spot, side = me >> 1, me & 1
    near = spot < 2
    there = [
        spot,
        spot ^ 1,
        jnp.where(near, 2, 1),
        jnp.where(near, 3, 0),
    ][slot]
    return 2 * there + side


def correlate_kernel(rows, two, aliased, scale, me_ref, *refs):
    refs = list(refs)
    hankels = [refs.pop(0) for _ in range(rows)]
    first = refs.pop(0)
    second = refs.pop(0) if two else None
    if aliased:
        refs.pop(0)
    held = refs.pop()
    out_ref = refs.pop(0)
    depth, width = first.shape
    step = pl.program_id(0)
    each = hankels[0].shape[0] // ROWS

    @pl.when(step == 0)
    def _():
        held[depth:] = jnp.zeros((held.shape[0] - depth, width), held.dtype)
        if two:
            end = at_end(me_ref[0] >> 1)

            @pl.when(end)
            def _():
                held[:depth] = first[...]

            @pl.when(jnp.logical_not(end))
            def _():
                held[:depth] = second[...]
        else:
            held[:depth] = first[...]

    def product(ref, at):
        lagged = ref[pl.ds(pl.multiple_of(at * ROWS, ROWS), ROWS), :]
        return jnp.dot(lagged, held[...], preferred_element_type=jnp.float32) * scale

    if rows == 1:
        out_ref[...] = product(hankels[0], step).reshape(out_ref.shape).astype(out_ref.dtype)
        return
    sent_ref = refs.pop(0)

    @pl.when(step < each)
    def _():
        sent_ref[...] = product(hankels[1], step).reshape(sent_ref.shape).astype(sent_ref.dtype)

    @pl.when(step >= each)
    def _():
        out_ref[...] = product(hankels[0], step - each).reshape(out_ref.shape)


def correlate(hankels, operands, me, place, scale, out, channels, sent=False):
    lanes, span = hankels[0].shape
    sources = lanes // LAGS
    depth, width = operands[0].shape
    group = ROWS // LAGS
    each = lanes // ROWS
    rows = len(hankels)
    skip = (rows - 1) * each
    resident = pl.BlockSpec(memory_space=pltpu.VMEM)
    in_specs = [resident] * rows
    in_specs += [pl.BlockSpec((depth, width), lambda i, me: (0, 0))] * len(operands)
    arguments = [*hankels, *operands]
    aliases = {}
    if out is not None and not sent:
        in_specs.append(pl.BlockSpec(memory_space=pl.ANY))
        arguments.append(out)
        aliases = {len(arguments): 0}
    sent_shape = jax.ShapeDtypeStruct((sources, LAGS, width), jnp.bfloat16)
    sent_spec = pl.BlockSpec((group, LAGS, width), lambda i, me: (jnp.minimum(i, each - 1), 0, 0))
    out_shape = [jax.ShapeDtypeStruct((1, sources, LAGS, channels), jnp.float32)]
    out_specs = [
        pl.BlockSpec(
            (pl.Element(1), pl.Element(group), pl.Element(LAGS), pl.Element(width)),
            lambda i, me: (
                0,
                jnp.maximum(i - skip, 0) * group,
                0,
                pl.multiple_of(place(me[0]), 128),
            ),
        )
    ]
    if rows == 2:
        out_shape.append(sent_shape)
        out_specs.append(sent_spec)
    if sent:
        out_shape, out_specs = [sent_shape], [sent_spec]
    return pl.pallas_call(
        functools.partial(correlate_kernel, rows, len(operands) == 2, bool(aliases), scale),
        out_shape=out_shape,
        grid_spec=pltpu.PrefetchScalarGridSpec(
            num_scalar_prefetch=1,
            grid=(rows * each,),
            in_specs=in_specs,
            out_specs=out_specs,
            scratch_shapes=[pltpu.VMEM((span, width), jnp.bfloat16)],
        ),
        input_output_aliases=aliases,
        compiler_params=params(),
        cost_estimate=pl.CostEstimate(
            flops=2 * rows * lanes * span * width,
            bytes_accessed=2 * depth * width + 4 * lanes * width,
            transcendentals=0,
        ),
        name="correlate",
    )(me, *arguments)


def store_kernel(me_ref, got_ref, kept_ref, out_ref):
    out_ref[...] = got_ref[...].astype(jnp.float32)[None]


def store(got, me, place, out):
    sources, lags, width = got.shape
    group = ROWS // LAGS
    return pl.pallas_call(
        store_kernel,
        out_shape=jax.ShapeDtypeStruct(out.shape, out.dtype),
        grid_spec=pltpu.PrefetchScalarGridSpec(
            num_scalar_prefetch=1,
            grid=(sources // group,),
            in_specs=[
                pl.BlockSpec((group, lags, width), lambda i, me: (i, 0, 0)),
                pl.BlockSpec(memory_space=pl.ANY),
            ],
            out_specs=pl.BlockSpec(
                (pl.Element(1), pl.Element(group), pl.Element(lags), pl.Element(width)),
                lambda i, me: (0, i * group, 0, pl.multiple_of(place(me[0]), 128)),
            ),
        ),
        input_output_aliases={2: 0},
        compiler_params=params(),
        cost_estimate=pl.CostEstimate(
            flops=0, bytes_accessed=6 * sources * lags * width, transcendentals=0
        ),
        name="store",
    )(me, got, out)


def hop(array, pairs):
    return lax.ppermute(array, "src", pairs)


def line_of_four(strain, dead_mask, src_index):
    samples, channels = strain.shape
    devices = lax.axis_size("src")
    line = devices // 2
    count = len(WIDTHS)
    offsets = [sum(WIDTHS[:c]) for c in range(count)]
    total = channels * devices
    own = src_index.shape[0] // devices
    scale = 1.0 / math.sqrt(samples)
    me = lax.axis_index("src")

    def along(pairs):
        return [(2 * a + s, 2 * b + s) for a, b in pairs for s in range(2)]

    outer = along([(0, 1), (1, 0), (2, 3), (3, 2)])
    inner = along([(1, 2), (2, 1)])
    outward = along([(1, 0), (2, 3)])
    across = [(i, i ^ 1) for i in range(devices)]

    def masked(rows):
        return jnp.where(dead_mask > 0, rows, jnp.zeros((), rows.dtype))

    lead = passed_along(masked(strain[samples - HALF :]), "win", 1)
    trail = passed_along(masked(strain[:SPAN]), "win", -1)
    alive = (dead_mask > 0).astype(jnp.int32)
    flats = []
    for c in range(count):
        flats.append(
            normalize_chunk(strain, alive, lead, trail, offsets[c], WIDTHS[c])
        )

    here = jnp.reshape(me, (1,)).astype(jnp.int32)
    theirs, mine = select_sources(flats, src_index, here, samples, own)
    heard = hop(theirs, across)
    blocks = [
        mine[by * own : (by + 1) * own] + heard[by * own : (by + 1) * own] for by in range(line)
    ]
    traces = blocks[0]
    for by in range(1, line):
        traces = traces + hop(blocks[by], along([(i, (i + by) % line) for i in range(line)]))
    partner_traces = hop(traces, across)
    own_rows = hankel(traces)
    partner_rows = hankel(partner_traces)

    def hops(arrays, pairs):
        return [hop(a, pairs) for a in arrays]

    first_out = hops(flats, outer)
    first_in = hops(flats, inner)
    swapped = hop(flats[0], across)
    second_out = hops(first_in, outward)
    second_in = hops(first_out, inner)
    third_out = hops(second_in, outward)

    arrivals = [
        [[f] for f in flats],
        [[f] for f in first_out],
        [list(pair) for pair in zip(second_out, first_in)],
        [list(pair) for pair in zip(third_out, second_in)],
    ]
    out = None
    waiting = []

    def place(slot, c, partner):
        return lambda me: (origin(slot, me) ^ partner) * channels + offsets[c]

    def add(slot, c, partner, chunk, hankels):
        nonlocal out
        out, *sent = correlate(
            hankels, chunk, here, place(slot, c, partner), scale, out, total
        )
        return sent

    def keep():
        nonlocal out
        out = store(*waiting.pop(0), out)

    add(0, 0, 0, [flats[0]], [own_rows])
    for slot, c in STEPS:
        chunk = arrivals[slot][c]
        if slot < line - 1:
            (made,) = add(slot, c, 0, chunk, [own_rows, partner_rows])
        else:
            (made,) = correlate(
                [partner_rows], chunk, here, place(slot, c, 0), scale, out, total, sent=True
            )
            add(slot, c, 0, chunk, [own_rows])
        waiting.append((hop(made, across), here, place(slot, c, 1)))
        if (slot, c) == (0, count - 1):
            add(0, 0, 1, [swapped], [own_rows])
        for _ in range(STORED.get((slot, c), 0)):
            keep()
    while waiting:
        keep()
    return out


def gathered(strain, dead_mask, src_index):
    samples, channels = strain.shape
    devices = lax.axis_size("src")
    scale = 1.0 / math.sqrt(samples)
    masked = jnp.where(dead_mask > 0, strain, jnp.zeros((), strain.dtype))
    lead = passed_along(masked[samples - HALF :], "win", 1)
    trail = passed_along(masked[:SPAN], "win", -1)
    rows = jnp.concatenate([lead, masked, trail], axis=0).astype(jnp.float32)
    sums = lax.reduce_window(
        jnp.abs(rows), jnp.zeros((), jnp.float32), lax.add, (2 * HALF + 1, 1), (1, 1), "VALID"
    )
    center = rows[HALF : rows.shape[0] - HALF]
    flat = (center / (sums / (2 * HALF + 1) + EPSILON)).astype(jnp.bfloat16)
    offset = lax.axis_index("src") * channels
    onehot = (src_index[:, None] - offset == jnp.arange(channels, dtype=jnp.int32)[None, :]).astype(
        jnp.bfloat16
    )
    selected = lax.dot_general(
        onehot, flat[:samples], (((1,), (1,)), ((), ())), preferred_element_type=jnp.float32
    )
    traces = lax.psum_scatter(
        selected.astype(jnp.bfloat16), "src", scatter_dimension=0, tiled=True
    )
    sources = traces.shape[0]
    tail = flat.shape[0] - samples
    shifted = [jnp.pad(traces, ((0, 0), (lag, tail - lag))) for lag in range(LAGS)]
    lagged = jnp.stack(shifted, axis=1).reshape(sources * LAGS, flat.shape[0])
    everywhere = lax.all_gather(flat, "src", axis=1, tiled=True)
    joined = jnp.dot(lagged, everywhere, preferred_element_type=jnp.float32) * scale
    return joined.reshape(1, sources, LAGS, channels * devices)


def lined(devices, channels):
    return devices == 8 and channels == sum(WIDTHS)


def shards(strain, dead_mask, src_index):
    if lined(lax.axis_size("src"), strain.shape[1]):
        return line_of_four(strain, dead_mask, src_index)
    return gathered(strain, dead_mask, src_index)


def solution(mesh):
    in_specs = (P("win", "src"), P("win", "src"), P())
    out_specs = P("win", "src", None, None)
    return jax.shard_map(shards, mesh=mesh, in_specs=in_specs, out_specs=out_specs, check_vma=False)
```

```python
import functools
import math

import jax
import jax.numpy as jnp
from jax import lax
from jax.experimental import pallas as pl
from jax.experimental.pallas import tpu as pltpu
from jax.sharding import PartitionSpec as P


LAGS = 32
HALF = 32
EPSILON = 1e-05
TILE = 192
SPAN = 2 * HALF
ROWS = 512
VMEM_BYTES = 24 << 20

WIDTHS = (384, 384, 256, 128, 128)
EARLY = (0, 1, 2, 3, 4)
LATE = (0, 1, 2, 3, 4)
STEPS = (
    [(0, c) for c in EARLY[1:]]
    + [(1, c) for c in EARLY]
    + [(2, c) for c in LATE]
    + [(3, c) for c in LATE]
)
STORED = {(1, 4): 5, (2, 0): 3, (2, 1): 1, (2, 2): 1, (2, 4): 3, (3, 0): 2, (3, 3): 1}


def passed_along(array, axis, by):
    devices = lax.axis_size(axis)
    pairs = [(i, i + by) for i in range(devices) if 0 <= i + by < devices]
    return lax.ppermute(array, axis, pairs)


def normalize_kernel(offset, strain_ref, mask_ref, lead_ref, trail_ref, flat_ref, held, rows):
    samples = strain_ref.shape[0]
    columns = pl.ds(offset, flat_ref.shape[1])
    pltpu.sync_copy(strain_ref.at[:, columns], held)
    alive = jnp.broadcast_to(mask_ref[...] > 0, held.shape)
    rows[:HALF] = lead_ref[...]
    rows[HALF : HALF + samples] = jnp.where(
        alive, held[...].astype(jnp.float32), 0.0
    ).astype(jnp.bfloat16)
    rows[HALF + samples :] = trail_ref[...]
    out_rows = flat_ref.shape[0]
    row = lax.broadcasted_iota(jnp.int32, (TILE, TILE + SPAN), 0)
    col = lax.broadcasted_iota(jnp.int32, (TILE, TILE + SPAN), 1)
    band = jnp.where((col >= row) & (col <= row + SPAN), 1.0, 0.0).astype(jnp.bfloat16)
    for start in range(0, out_rows, TILE):
        count = min(TILE, out_rows - start)
        near = rows[start : start + count + SPAN]
        sums = jnp.dot(
            band[:count, : count + SPAN], jnp.abs(near), preferred_element_type=jnp.float32
        )
        center = rows[start + HALF : start + HALF + count].astype(jnp.float32)
        flat_ref[start : start + count] = (
            center / (sums / (2 * HALF + 1) + EPSILON)
        ).astype(jnp.bfloat16)


def params():
    return pltpu.CompilerParams(vmem_limit_bytes=VMEM_BYTES)


def normalize_chunk(strain, mask, lead, trail, offset, width):
    samples = strain.shape[0]

    def block(rows):
        return pl.BlockSpec((pl.Element(rows), pl.Element(width)), lambda i: (0, offset))

    return pl.pallas_call(
        functools.partial(normalize_kernel, offset),
        out_shape=jax.ShapeDtypeStruct((samples + HALF, width), jnp.bfloat16),
        grid=(1,),
        in_specs=[pl.BlockSpec(memory_space=pltpu.HBM), block(1), block(HALF), block(SPAN)],
        out_specs=pl.BlockSpec((samples + HALF, width), lambda i: (0, 0)),
        scratch_shapes=[
            pltpu.VMEM((samples, width), jnp.bfloat16),
            pltpu.VMEM((samples + HALF + SPAN, width), jnp.bfloat16),
        ],
        compiler_params=pltpu.CompilerParams(vmem_limit_bytes=52 << 20),
        cost_estimate=pl.CostEstimate(
            flops=2 * (samples + HALF) * (TILE + SPAN) * width,
            bytes_accessed=4 * samples * width,
            transcendentals=0,
        ),
        name="normalize",
    )(strain, mask, lead, trail)


def select_kernel(own, me_ref, index_ref, *refs):
    flats, (theirs_ref, mine_ref) = refs[:-2], refs[-2:]
    half = theirs_ref.shape[0]
    me = me_ref[0]
    spot, side = me >> 1, me & 1
    line = half // own
    index = jnp.concatenate(
        [
            index_ref[pl.ds(pl.multiple_of(block * own, own), own), :]
            for far in (1, 0)
            for block in [
                2 * ((spot + by) & (line - 1)) + (side ^ far) for by in range(line)
            ]
        ],
        axis=0,
    )
    offset = me * sum(flat.shape[1] for flat in flats)
    total = jnp.zeros((2 * half, theirs_ref.shape[1]), jnp.float32)
    for flat_ref in flats:
        width = flat_ref.shape[1]
        channel = lax.broadcasted_iota(jnp.int32, (2 * half, width), 1) + offset
        onehot = jnp.where(index == channel, 1.0, 0.0).astype(jnp.bfloat16)
        total += lax.dot_general(
            onehot, flat_ref[...], (((1,), (1,)), ((), ())), preferred_element_type=jnp.float32
        )
        offset += width
    theirs_ref[...] = total[:half].astype(jnp.bfloat16)
    mine_ref[...] = total[half:].astype(jnp.bfloat16)


def select_sources(flats, index, me, samples, own):
    sources = index.shape[0]
    channels = sum(f.shape[1] for f in flats)
    return pl.pallas_call(
        functools.partial(select_kernel, own),
        out_shape=[jax.ShapeDtypeStruct((sources // 2, samples), jnp.bfloat16)] * 2,
        grid_spec=pltpu.PrefetchScalarGridSpec(
            num_scalar_prefetch=1,
            grid=(samples // 256,),
            in_specs=[pl.BlockSpec((sources, 1), lambda i, me: (0, 0))]
            + [pl.BlockSpec((256, f.shape[1]), lambda i, me: (i, 0)) for f in flats],
            out_specs=[pl.BlockSpec((sources // 2, 256), lambda i, me: (0, i))] * 2,
        ),
        compiler_params=params(),
        cost_estimate=pl.CostEstimate(
            flops=2 * sources * samples * channels,
            bytes_accessed=2 * samples * channels,
            transcendentals=0,
        ),
        name="select",
    )(me, index[:, None], *flats)


def hankel_kernel(trace_ref, out_ref):
    width = out_ref.shape[1]
    for source in range(trace_ref.shape[0]):
        spread = jnp.broadcast_to(trace_ref[source : source + 1], (LAGS, width))
        shifted = pltpu.roll(spread, 0, 1, stride=1, stride_axis=0)
        out_ref[source * LAGS : (source + 1) * LAGS] = shifted.astype(jnp.bfloat16)


def hankel(traces):
    sources, samples = traces.shape
    width = samples + 128
    padded = jnp.pad(traces.astype(jnp.float32), ((0, 0), (0, 128)))
    return pl.pallas_call(
        hankel_kernel,
        out_shape=jax.ShapeDtypeStruct((sources * LAGS, width), jnp.bfloat16),
        grid=(sources // 8,),
        in_specs=[pl.BlockSpec((8, width), lambda i: (i, 0))],
        out_specs=pl.BlockSpec((8 * LAGS, width), lambda i: (i, 0)),
        compiler_params=params(),
        cost_estimate=pl.CostEstimate(
            flops=sources * LAGS * width, bytes_accessed=2 * sources * LAGS * width, transcendentals=0
        ),
        name="hankel",
    )(padded)


def at_end(spot):
    return (spot == 0) | (spot == 3)


def origin(slot, me):
    spot, side = me >> 1, me & 1
    near = spot < 2
    there = [
        spot,
        spot ^ 1,
        jnp.where(near, 2, 1),
        jnp.where(near, 3, 0),
    ][slot]
    return 2 * there + side


def correlate_kernel(rows, two, aliased, scale, me_ref, *refs):
    refs = list(refs)
    hankels = [refs.pop(0) for _ in range(rows)]
    first = refs.pop(0)
    second = refs.pop(0) if two else None
    if aliased:
        refs.pop(0)
    held = refs.pop()
    out_ref = refs.pop(0)
    depth, width = first.shape
    step = pl.program_id(0)
    each = hankels[0].shape[0] // ROWS

    @pl.when(step == 0)
    def _():
        held[depth:] = jnp.zeros((held.shape[0] - depth, width), held.dtype)
        if two:
            end = at_end(me_ref[0] >> 1)

            @pl.when(end)
            def _():
                held[:depth] = first[...]

            @pl.when(jnp.logical_not(end))
            def _():
                held[:depth] = second[...]
        else:
            held[:depth] = first[...]

    def product(ref, at):
        lagged = ref[pl.ds(pl.multiple_of(at * ROWS, ROWS), ROWS), :]
        return jnp.dot(lagged, held[...], preferred_element_type=jnp.float32) * scale

    if rows == 1:
        out_ref[...] = product(hankels[0], step).reshape(out_ref.shape).astype(out_ref.dtype)
        return
    sent_ref = refs.pop(0)

    @pl.when(step < each)
    def _():
        sent_ref[...] = product(hankels[1], step).reshape(sent_ref.shape).astype(sent_ref.dtype)

    @pl.when(step >= each)
    def _():
        out_ref[...] = product(hankels[0], step - each).reshape(out_ref.shape)


def correlate(hankels, operands, me, place, scale, out, channels, sent=False):
    lanes, span = hankels[0].shape
    sources = lanes // LAGS
    depth, width = operands[0].shape
    group = ROWS // LAGS
    each = lanes // ROWS
    rows = len(hankels)
    skip = (rows - 1) * each
    resident = pl.BlockSpec(memory_space=pltpu.VMEM)
    in_specs = [resident] * rows
    in_specs += [pl.BlockSpec((depth, width), lambda i, me: (0, 0))] * len(operands)
    arguments = [*hankels, *operands]
    aliases = {}
    if out is not None and not sent:
        in_specs.append(pl.BlockSpec(memory_space=pl.ANY))
        arguments.append(out)
        aliases = {len(arguments): 0}
    sent_shape = jax.ShapeDtypeStruct((sources, LAGS, width), jnp.bfloat16)
    sent_spec = pl.BlockSpec((group, LAGS, width), lambda i, me: (jnp.minimum(i, each - 1), 0, 0))
    out_shape = [jax.ShapeDtypeStruct((1, sources, LAGS, channels), jnp.float32)]
    out_specs = [
        pl.BlockSpec(
            (pl.Element(1), pl.Element(group), pl.Element(LAGS), pl.Element(width)),
            lambda i, me: (
                0,
                jnp.maximum(i - skip, 0) * group,
                0,
                pl.multiple_of(place(me[0]), 128),
            ),
        )
    ]
    if rows == 2:
        out_shape.append(sent_shape)
        out_specs.append(sent_spec)
    if sent:
        out_shape, out_specs = [sent_shape], [sent_spec]
    return pl.pallas_call(
        functools.partial(correlate_kernel, rows, len(operands) == 2, bool(aliases), scale),
        out_shape=out_shape,
        grid_spec=pltpu.PrefetchScalarGridSpec(
            num_scalar_prefetch=1,
            grid=(rows * each,),
            in_specs=in_specs,
            out_specs=out_specs,
            scratch_shapes=[pltpu.VMEM((span, width), jnp.bfloat16)],
        ),
        input_output_aliases=aliases,
        compiler_params=params(),
        cost_estimate=pl.CostEstimate(
            flops=2 * rows * lanes * span * width,
            bytes_accessed=2 * depth * width + 4 * lanes * width,
            transcendentals=0,
        ),
        name="correlate",
    )(me, *arguments)


def store_kernel(me_ref, got_ref, kept_ref, out_ref):
    out_ref[...] = got_ref[...].astype(jnp.float32)[None]


def store(got, me, place, out):
    sources, lags, width = got.shape
    group = ROWS // LAGS
    return pl.pallas_call(
        store_kernel,
        out_shape=jax.ShapeDtypeStruct(out.shape, out.dtype),
        grid_spec=pltpu.PrefetchScalarGridSpec(
            num_scalar_prefetch=1,
            grid=(sources // group,),
            in_specs=[
                pl.BlockSpec((group, lags, width), lambda i, me: (i, 0, 0)),
                pl.BlockSpec(memory_space=pl.ANY),
            ],
            out_specs=pl.BlockSpec(
                (pl.Element(1), pl.Element(group), pl.Element(lags), pl.Element(width)),
                lambda i, me: (0, i * group, 0, pl.multiple_of(place(me[0]), 128)),
            ),
        ),
        input_output_aliases={2: 0},
        compiler_params=params(),
        cost_estimate=pl.CostEstimate(
            flops=0, bytes_accessed=6 * sources * lags * width, transcendentals=0
        ),
        name="store",
    )(me, got, out)


def hop(array, pairs):
    return lax.ppermute(array, "src", pairs)


def line_of_four(strain, dead_mask, src_index):
    samples, channels = strain.shape
    devices = lax.axis_size("src")
    line = devices // 2
    count = len(WIDTHS)
    offsets = [sum(WIDTHS[:c]) for c in range(count)]
    total = channels * devices
    own = src_index.shape[0] // devices
    scale = 1.0 / math.sqrt(samples)
    me = lax.axis_index("src")

    def along(pairs):
        return [(2 * a + s, 2 * b + s) for a, b in pairs for s in range(2)]

    outer = along([(0, 1), (1, 0), (2, 3), (3, 2)])
    inner = along([(1, 2), (2, 1)])
    outward = along([(1, 0), (2, 3)])
    across = [(i, i ^ 1) for i in range(devices)]

    def masked(rows):
        return jnp.where(dead_mask > 0, rows, jnp.zeros((), rows.dtype))

    lead = passed_along(masked(strain[samples - HALF :]), "win", 1)
    trail = passed_along(masked(strain[:SPAN]), "win", -1)
    alive = (dead_mask > 0).astype(jnp.int32)
    flats = []
    for c in range(count):
        flats.append(
            normalize_chunk(strain, alive, lead, trail, offsets[c], WIDTHS[c])
        )

    here = jnp.reshape(me, (1,)).astype(jnp.int32)
    theirs, mine = select_sources(flats, src_index, here, samples, own)
    heard = hop(theirs, across)
    blocks = [
        mine[by * own : (by + 1) * own] + heard[by * own : (by + 1) * own] for by in range(line)
    ]
    traces = blocks[0]
    for by in range(1, line):
        traces = traces + hop(blocks[by], along([(i, (i + by) % line) for i in range(line)]))
    partner_traces = hop(traces, across)
    own_rows = hankel(traces)
    partner_rows = hankel(partner_traces)

    def hops(arrays, pairs):
        return [hop(a, pairs) for a in arrays]

    first_out = hops(flats, outer)
    first_in = hops(flats, inner)
    swapped = hop(flats[0], across)
    second_out = hops(first_in, outward)
    second_in = hops(first_out, inner)
    third_out = hops(second_in, outward)

    arrivals = [
        [[f] for f in flats],
        [[f] for f in first_out],
        [list(pair) for pair in zip(second_out, first_in)],
        [list(pair) for pair in zip(third_out, second_in)],
    ]
    out = None
    waiting = []

    def place(slot, c, partner):
        return lambda me: (origin(slot, me) ^ partner) * channels + offsets[c]

    def add(slot, c, partner, chunk, hankels):
        nonlocal out
        out, *sent = correlate(
            hankels, chunk, here, place(slot, c, partner), scale, out, total
        )
        return sent

    def keep():
        nonlocal out
        out = store(*waiting.pop(0), out)

    add(0, 0, 0, [flats[0]], [own_rows])
    for slot, c in STEPS:
        chunk = arrivals[slot][c]
        if slot < line - 1:
            (made,) = add(slot, c, 0, chunk, [own_rows, partner_rows])
        else:
            (made,) = correlate(
                [partner_rows], chunk, here, place(slot, c, 0), scale, out, total, sent=True
            )
            add(slot, c, 0, chunk, [own_rows])
        waiting.append((hop(made, across), here, place(slot, c, 1)))
        if (slot, c) == (0, count - 1):
            add(0, 0, 1, [swapped], [own_rows])
        for _ in range(STORED.get((slot, c), 0)):
            keep()
    while waiting:
        keep()
    return out


def gathered(strain, dead_mask, src_index):
    samples, channels = strain.shape
    devices = lax.axis_size("src")
    scale = 1.0 / math.sqrt(samples)
    masked = jnp.where(dead_mask > 0, strain, jnp.zeros((), strain.dtype))
    lead = passed_along(masked[samples - HALF :], "win", 1)
    trail = passed_along(masked[:SPAN], "win", -1)
    rows = jnp.concatenate([lead, masked, trail], axis=0).astype(jnp.float32)
    sums = lax.reduce_window(
        jnp.abs(rows), jnp.zeros((), jnp.float32), lax.add, (2 * HALF + 1, 1), (1, 1), "VALID"
    )
    center = rows[HALF : rows.shape[0] - HALF]
    flat = (center / (sums / (2 * HALF + 1) + EPSILON)).astype(jnp.bfloat16)
    offset = lax.axis_index("src") * channels
    onehot = (src_index[:, None] - offset == jnp.arange(channels, dtype=jnp.int32)[None, :]).astype(
        jnp.bfloat16
    )
    selected = lax.dot_general(
        onehot, flat[:samples], (((1,), (1,)), ((), ())), preferred_element_type=jnp.float32
    )
    traces = lax.psum_scatter(
        selected.astype(jnp.bfloat16), "src", scatter_dimension=0, tiled=True
    )
    sources = traces.shape[0]
    tail = flat.shape[0] - samples
    shifted = [jnp.pad(traces, ((0, 0), (lag, tail - lag))) for lag in range(LAGS)]
    lagged = jnp.stack(shifted, axis=1).reshape(sources * LAGS, flat.shape[0])
    everywhere = lax.all_gather(flat, "src", axis=1, tiled=True)
    joined = jnp.dot(lagged, everywhere, preferred_element_type=jnp.float32) * scale
    return joined.reshape(1, sources, LAGS, channels * devices)


def lined(devices, channels):
    return devices == 8 and channels == sum(WIDTHS)


def shards(strain, dead_mask, src_index):
    if lined(lax.axis_size("src"), strain.shape[1]):
        return line_of_four(strain, dead_mask, src_index)
    return gathered(strain, dead_mask, src_index)


def solution(mesh):
    in_specs = (P("win", "src"), P("win", "src"), P())
    out_specs = P("win", "src", None, None)
    return jax.shard_map(shards, mesh=mesh, in_specs=in_specs, out_specs=out_specs, check_vma=False)
```

```python
import functools
import math

import jax
import jax.numpy as jnp
from jax import lax
from jax.experimental import pallas as pl
from jax.experimental.pallas import tpu as pltpu
from jax.sharding import PartitionSpec as P


LAGS = 32
HALF = 32
EPSILON = 1e-05
TILE = 192
SPAN = 2 * HALF
ROWS = 512
VMEM_BYTES = 24 << 20

WIDTHS = (384, 512, 256, 128)
EARLY = (0, 1, 2, 3)
LATE = (1, 0, 2, 3)
SHARED = 2
STEPS = (
    [(0, c) for c in LATE if c != SHARED]
    + [(1, c) for c in EARLY]
    + [(2, c) for c in LATE]
    + [(3, c) for c in LATE]
)
STORED = {(1, 3): 4, (2, 1): 3, (2, 2): 1, (2, 3): 3, (3, 0): 1}


def passed_along(array, axis, by):
    devices = lax.axis_size(axis)
    pairs = [(i, i + by) for i in range(devices) if 0 <= i + by < devices]
    return lax.ppermute(array, axis, pairs)


def normalize_kernel(offset, masks, strain_ref, *refs):
    mask_ref = refs[0] if masks else None
    lead_ref, trail_ref, flat_ref, held, rows = refs[masks:]
    samples = strain_ref.shape[0]
    columns = pl.ds(offset, flat_ref.shape[1])
    pltpu.sync_copy(strain_ref.at[:, columns], held)
    if masks:
        alive = jnp.broadcast_to(mask_ref[...] > 0, held.shape)
        rows[HALF : HALF + samples] = jnp.where(
            alive, held[...].astype(jnp.float32), 0.0
        ).astype(jnp.bfloat16)
    else:
        rows[HALF : HALF + samples] = held[...]
    rows[:HALF] = lead_ref[...]
    rows[HALF + samples :] = trail_ref[...]
    out_rows = flat_ref.shape[0]
    row = lax.broadcasted_iota(jnp.int32, (TILE, TILE + SPAN), 0)
    col = lax.broadcasted_iota(jnp.int32, (TILE, TILE + SPAN), 1)
    band = jnp.where((col >= row) & (col <= row + SPAN), 1.0, 0.0).astype(jnp.bfloat16)
    for start in range(0, out_rows, TILE):
        count = min(TILE, out_rows - start)
        near = rows[start : start + count + SPAN]
        sums = jnp.dot(
            band[:count, : count + SPAN], jnp.abs(near), preferred_element_type=jnp.float32
        )
        center = rows[start + HALF : start + HALF + count].astype(jnp.float32)
        flat_ref[start : start + count] = (
            center / (sums / (2 * HALF + 1) + EPSILON)
        ).astype(jnp.bfloat16)


def params():
    return pltpu.CompilerParams(vmem_limit_bytes=VMEM_BYTES)


def normalize_chunk(strain, mask, lead, trail, offset, width):
    samples = strain.shape[0]
    masks = [] if mask is None else [mask]

    def block(rows):
        return pl.BlockSpec((pl.Element(rows), pl.Element(width)), lambda i: (0, offset))

    return pl.pallas_call(
        functools.partial(normalize_kernel, offset, len(masks)),
        out_shape=jax.ShapeDtypeStruct((samples + HALF, width), jnp.bfloat16),
        grid=(1,),
        in_specs=[pl.BlockSpec(memory_space=pltpu.HBM)]
        + [block(1)] * len(masks)
        + [block(HALF), block(SPAN)],
        out_specs=pl.BlockSpec((samples + HALF, width), lambda i: (0, 0)),
        scratch_shapes=[
            pltpu.VMEM((samples, width), jnp.bfloat16),
            pltpu.VMEM((samples + HALF + SPAN, width), jnp.bfloat16),
        ],
        compiler_params=pltpu.CompilerParams(vmem_limit_bytes=52 << 20),
        cost_estimate=pl.CostEstimate(
            flops=2 * (samples + HALF) * (TILE + SPAN) * width,
            bytes_accessed=4 * samples * width,
            transcendentals=0,
        ),
        name="normalize",
    )(strain, *masks, lead, trail)


def select_kernel(own, me_ref, index_ref, *refs):
    flats, (theirs_ref, mine_ref) = refs[:-2], refs[-2:]
    half = theirs_ref.shape[0]
    me = me_ref[0]
    spot, side = me >> 1, me & 1
    line = half // own
    index = jnp.concatenate(
        [
            index_ref[pl.ds(pl.multiple_of(block * own, own), own), :]
            for far in (1, 0)
            for block in [
                2 * ((spot + by) & (line - 1)) + (side ^ far) for by in range(line)
            ]
        ],
        axis=0,
    )
    offset = me * sum(flat.shape[1] for flat in flats)
    total = jnp.zeros((2 * half, theirs_ref.shape[1]), jnp.float32)
    for flat_ref in flats:
        width = flat_ref.shape[1]
        channel = lax.broadcasted_iota(jnp.int32, (2 * half, width), 1) + offset
        onehot = jnp.where(index == channel, 1.0, 0.0).astype(jnp.bfloat16)
        total += lax.dot_general(
            onehot, flat_ref[...], (((1,), (1,)), ((), ())), preferred_element_type=jnp.float32
        )
        offset += width
    theirs_ref[...] = total[:half].astype(jnp.bfloat16)
    mine_ref[...] = total[half:].astype(jnp.bfloat16)


def select_sources(flats, index, me, samples, own):
    sources = index.shape[0]
    channels = sum(f.shape[1] for f in flats)
    return pl.pallas_call(
        functools.partial(select_kernel, own),
        out_shape=[jax.ShapeDtypeStruct((sources // 2, samples), jnp.bfloat16)] * 2,
        grid_spec=pltpu.PrefetchScalarGridSpec(
            num_scalar_prefetch=1,
            grid=(samples // 256,),
            in_specs=[pl.BlockSpec((sources, 1), lambda i, me: (0, 0))]
            + [pl.BlockSpec((256, f.shape[1]), lambda i, me: (i, 0)) for f in flats],
            out_specs=[pl.BlockSpec((sources // 2, 256), lambda i, me: (0, i))] * 2,
        ),
        compiler_params=params(),
        cost_estimate=pl.CostEstimate(
            flops=2 * sources * samples * channels,
            bytes_accessed=2 * samples * channels,
            transcendentals=0,
        ),
        name="select",
    )(me, index[:, None], *flats)


def hankel_kernel(trace_ref, out_ref):
    width = out_ref.shape[1]
    for source in range(trace_ref.shape[0]):
        spread = jnp.broadcast_to(trace_ref[source : source + 1], (LAGS, width))
        shifted = pltpu.roll(spread, 0, 1, stride=1, stride_axis=0)
        out_ref[source * LAGS : (source + 1) * LAGS] = shifted.astype(jnp.bfloat16)


def hankel(traces):
    sources, samples = traces.shape
    width = samples + 128
    padded = jnp.pad(traces.astype(jnp.float32), ((0, 0), (0, 128)))
    return pl.pallas_call(
        hankel_kernel,
        out_shape=jax.ShapeDtypeStruct((sources * LAGS, width), jnp.bfloat16),
        grid=(sources // 8,),
        in_specs=[pl.BlockSpec((8, width), lambda i: (i, 0))],
        out_specs=pl.BlockSpec((8 * LAGS, width), lambda i: (i, 0)),
        compiler_params=params(),
        cost_estimate=pl.CostEstimate(
            flops=sources * LAGS * width, bytes_accessed=2 * sources * LAGS * width, transcendentals=0
        ),
        name="hankel",
    )(padded)


def at_end(spot):
    return (spot == 0) | (spot == 3)


def origin(slot, me):
    spot, side = me >> 1, me & 1
    near = spot < 2
    there = [
        spot,
        spot ^ 1,
        jnp.where(near, 2, 1),
        jnp.where(near, 3, 0),
    ][slot]
    return 2 * there + side


def correlate_kernel(rows, two, aliased, scale, me_ref, *refs):
    refs = list(refs)
    hankels = [refs.pop(0) for _ in range(rows)]
    first = refs.pop(0)
    second = refs.pop(0) if two else None
    if aliased:
        refs.pop(0)
    held = refs.pop()
    out_ref = refs.pop(0)
    depth, width = first.shape
    step = pl.program_id(0)
    each = hankels[0].shape[0] // ROWS

    @pl.when(step == 0)
    def _():
        held[depth:] = jnp.zeros((held.shape[0] - depth, width), held.dtype)
        if two:
            end = at_end(me_ref[0] >> 1)

            @pl.when(end)
            def _():
                held[:depth] = first[...]

            @pl.when(jnp.logical_not(end))
            def _():
                held[:depth] = second[...]
        else:
            held[:depth] = first[...]

    def product(ref, at):
        lagged = ref[pl.ds(pl.multiple_of(at * ROWS, ROWS), ROWS), :]
        return jnp.dot(lagged, held[...], preferred_element_type=jnp.float32) * scale

    if rows == 1:
        out_ref[...] = product(hankels[0], step).reshape(out_ref.shape).astype(out_ref.dtype)
        return
    sent_ref = refs.pop(0)

    @pl.when(step < each)
    def _():
        sent_ref[...] = product(hankels[1], step).reshape(sent_ref.shape).astype(sent_ref.dtype)

    @pl.when(step >= each)
    def _():
        out_ref[...] = product(hankels[0], step - each).reshape(out_ref.shape)


def correlate(hankels, operands, me, place, scale, out, channels, sent=False):
    lanes, span = hankels[0].shape
    sources = lanes // LAGS
    depth, width = operands[0].shape
    group = ROWS // LAGS
    each = lanes // ROWS
    rows = len(hankels)
    skip = (rows - 1) * each
    resident = pl.BlockSpec(memory_space=pltpu.VMEM)
    in_specs = [resident] * rows
    in_specs += [pl.BlockSpec((depth, width), lambda i, me: (0, 0))] * len(operands)
    arguments = [*hankels, *operands]
    aliases = {}
    if out is not None and not sent:
        in_specs.append(pl.BlockSpec(memory_space=pl.ANY))
        arguments.append(out)
        aliases = {len(arguments): 0}
    sent_shape = jax.ShapeDtypeStruct((sources, LAGS, width), jnp.bfloat16)
    sent_spec = pl.BlockSpec((group, LAGS, width), lambda i, me: (jnp.minimum(i, each - 1), 0, 0))
    out_shape = [jax.ShapeDtypeStruct((1, sources, LAGS, channels), jnp.float32)]
    out_specs = [
        pl.BlockSpec(
            (pl.Element(1), pl.Element(group), pl.Element(LAGS), pl.Element(width)),
            lambda i, me: (
                0,
                jnp.maximum(i - skip, 0) * group,
                0,
                pl.multiple_of(place(me[0]), 128),
            ),
        )
    ]
    if rows == 2:
        out_shape.append(sent_shape)
        out_specs.append(sent_spec)
    if sent:
        out_shape, out_specs = [sent_shape], [sent_spec]
    return pl.pallas_call(
        functools.partial(correlate_kernel, rows, len(operands) == 2, bool(aliases), scale),
        out_shape=out_shape,
        grid_spec=pltpu.PrefetchScalarGridSpec(
            num_scalar_prefetch=1,
            grid=(rows * each,),
            in_specs=in_specs,
            out_specs=out_specs,
            scratch_shapes=[pltpu.VMEM((span, width), jnp.bfloat16)],
        ),
        input_output_aliases=aliases,
        compiler_params=params(),
        cost_estimate=pl.CostEstimate(
            flops=2 * rows * lanes * span * width,
            bytes_accessed=2 * depth * width + 4 * lanes * width,
            transcendentals=0,
        ),
        name="correlate",
    )(me, *arguments)


def store_kernel(me_ref, got_ref, kept_ref, out_ref):
    out_ref[...] = got_ref[...].astype(jnp.float32)[None]


def store(got, me, place, out):
    sources, lags, width = got.shape
    group = ROWS // LAGS
    return pl.pallas_call(
        store_kernel,
        out_shape=jax.ShapeDtypeStruct(out.shape, out.dtype),
        grid_spec=pltpu.PrefetchScalarGridSpec(
            num_scalar_prefetch=1,
            grid=(sources // group,),
            in_specs=[
                pl.BlockSpec((group, lags, width), lambda i, me: (i, 0, 0)),
                pl.BlockSpec(memory_space=pl.ANY),
            ],
            out_specs=pl.BlockSpec(
                (pl.Element(1), pl.Element(group), pl.Element(lags), pl.Element(width)),
                lambda i, me: (0, i * group, 0, pl.multiple_of(place(me[0]), 128)),
            ),
        ),
        input_output_aliases={2: 0},
        compiler_params=params(),
        cost_estimate=pl.CostEstimate(
            flops=0, bytes_accessed=6 * sources * lags * width, transcendentals=0
        ),
        name="store",
    )(me, got, out)


def hop(array, pairs):
    return lax.ppermute(array, "src", pairs)


def line_of_four(strain, dead_mask, src_index):
    samples, channels = strain.shape
    devices = lax.axis_size("src")
    line = devices // 2
    count = len(WIDTHS)
    offsets = [sum(WIDTHS[:c]) for c in range(count)]
    total = channels * devices
    own = src_index.shape[0] // devices
    scale = 1.0 / math.sqrt(samples)
    me = lax.axis_index("src")

    def along(pairs):
        return [(2 * a + s, 2 * b + s) for a, b in pairs for s in range(2)]

    outer = along([(0, 1), (1, 0), (2, 3), (3, 2)])
    inner = along([(1, 2), (2, 1)])
    outward = along([(1, 0), (2, 3)])
    across = [(i, i ^ 1) for i in range(devices)]

    def masked(rows):
        return jnp.where(dead_mask > 0, rows, jnp.zeros((), rows.dtype))

    def around(rows):
        trail = passed_along(rows(0, SPAN), "win", -1)
        lead = passed_along(rows(samples - HALF, samples), "win", 1)
        return lead, trail

    raw = jnp.where(
        dead_mask[:, : WIDTHS[0]] > 0, strain[:, : WIDTHS[0]], jnp.zeros((), strain.dtype)
    )
    raw_out = hop(raw, outer)
    raw_in = hop(raw, inner)
    lead, trail = around(lambda a, b: masked(strain[a:b]))
    alive = (dead_mask > 0).astype(jnp.int32)
    flats = []
    for c in range(count):
        flats.append(
            normalize_chunk(strain, alive, lead, trail, offsets[c], WIDTHS[c])
        )

    here = jnp.reshape(me, (1,)).astype(jnp.int32)
    theirs, mine = select_sources(flats, src_index, here, samples, own)
    heard = hop(theirs, across)
    blocks = [
        mine[by * own : (by + 1) * own] + heard[by * own : (by + 1) * own] for by in range(line)
    ]
    traces = blocks[0]
    for by in range(1, line):
        traces = traces + hop(blocks[by], along([(i, (i + by) % line) for i in range(line)]))
    partner_traces = hop(traces, across)
    own_rows = hankel(traces)
    partner_rows = hankel(partner_traces)

    def hops(arrays, pairs):
        return [hop(a, pairs) for a in arrays]

    def received(chunk):
        before, after = around(lambda a, b: chunk[a:b])
        return normalize_chunk(chunk, None, before, after, 0, WIDTHS[0])

    first_out = [received(raw_out)]
    first_in = [received(raw_in)]
    first_out += [hop(flats[c], outer) for c in range(1, count)]
    first_in += [hop(flats[c], inner) for c in range(1, count)]
    swapped = hop(flats[SHARED], across)
    second_out = hops(first_in, outward)
    second_in = hops(first_out, inner)
    third_out = hops(second_in, outward)

    arrivals = [
        [[f] for f in flats],
        [[f] for f in first_out],
        [list(pair) for pair in zip(second_out, first_in)],
        [list(pair) for pair in zip(third_out, second_in)],
    ]
    out = None
    waiting = []

    def place(slot, c, partner):
        return lambda me: (origin(slot, me) ^ partner) * channels + offsets[c]

    def add(slot, c, partner, chunk, hankels):
        nonlocal out
        out, *sent = correlate(
            hankels, chunk, here, place(slot, c, partner), scale, out, total
        )
        return sent

    def keep():
        nonlocal out
        out = store(*waiting.pop(0), out)

    add(0, SHARED, 0, [flats[SHARED]], [own_rows])
    for slot, c in STEPS:
        chunk = arrivals[slot][c]
        if slot < line - 1:
            (made,) = add(slot, c, 0, chunk, [own_rows, partner_rows])
        else:
            (made,) = correlate(
                [partner_rows], chunk, here, place(slot, c, 0), scale, out, total, sent=True
            )
            add(slot, c, 0, chunk, [own_rows])
        waiting.append((hop(made, across), here, place(slot, c, 1)))
        if (slot, c) == (0, count - 1):
            add(0, SHARED, 1, [swapped], [own_rows])
        for _ in range(STORED.get((slot, c), 0)):
            keep()
    while waiting:
        keep()
    return out


def gathered(strain, dead_mask, src_index):
    samples, channels = strain.shape
    devices = lax.axis_size("src")
    scale = 1.0 / math.sqrt(samples)
    masked = jnp.where(dead_mask > 0, strain, jnp.zeros((), strain.dtype))
    lead = passed_along(masked[samples - HALF :], "win", 1)
    trail = passed_along(masked[:SPAN], "win", -1)
    rows = jnp.concatenate([lead, masked, trail], axis=0).astype(jnp.float32)
    sums = lax.reduce_window(
        jnp.abs(rows), jnp.zeros((), jnp.float32), lax.add, (2 * HALF + 1, 1), (1, 1), "VALID"
    )
    center = rows[HALF : rows.shape[0] - HALF]
    flat = (center / (sums / (2 * HALF + 1) + EPSILON)).astype(jnp.bfloat16)
    offset = lax.axis_index("src") * channels
    onehot = (src_index[:, None] - offset == jnp.arange(channels, dtype=jnp.int32)[None, :]).astype(
        jnp.bfloat16
    )
    selected = lax.dot_general(
        onehot, flat[:samples], (((1,), (1,)), ((), ())), preferred_element_type=jnp.float32
    )
    traces = lax.psum_scatter(
        selected.astype(jnp.bfloat16), "src", scatter_dimension=0, tiled=True
    )
    sources = traces.shape[0]
    tail = flat.shape[0] - samples
    shifted = [jnp.pad(traces, ((0, 0), (lag, tail - lag))) for lag in range(LAGS)]
    lagged = jnp.stack(shifted, axis=1).reshape(sources * LAGS, flat.shape[0])
    everywhere = lax.all_gather(flat, "src", axis=1, tiled=True)
    joined = jnp.dot(lagged, everywhere, preferred_element_type=jnp.float32) * scale
    return joined.reshape(1, sources, LAGS, channels * devices)


def lined(devices, channels):
    return devices == 8 and channels == sum(WIDTHS)


def shards(strain, dead_mask, src_index):
    if lined(lax.axis_size("src"), strain.shape[1]):
        return line_of_four(strain, dead_mask, src_index)
    return gathered(strain, dead_mask, src_index)


def solution(mesh):
    in_specs = (P("win", "src"), P("win", "src"), P())
    out_specs = P("win", "src", None, None)
    return jax.shard_map(shards, mesh=mesh, in_specs=in_specs, out_specs=out_specs, check_vma=False)
```

```python
import functools
import math

import jax
import jax.numpy as jnp
from jax import lax
from jax.experimental import pallas as pl
from jax.experimental.pallas import tpu as pltpu
from jax.sharding import PartitionSpec as P


LAGS = 32
HALF = 32
EPSILON = 1e-05
TILE = 192
SPAN = 2 * HALF
ROWS = 512
VMEM_BYTES = 24 << 20
NORMALIZE_BYTES = 50 << 20

WIDTHS = (384, 512, 256, 128)
EARLY = (0, 1, 2, 3)
LATE = (1, 0, 2, 3)
SHARED = 2
STEPS = (
    [(0, c) for c in LATE if c != SHARED]
    + [(1, c) for c in EARLY]
    + [(2, c) for c in LATE]
    + [(3, c) for c in LATE]
)
STORED = {(1, 3): 4, (2, 1): 3, (2, 2): 1, (2, 3): 3, (3, 0): 1}


def passed_along(array, axis, by):
    devices = lax.axis_size(axis)
    pairs = [(i, i + by) for i in range(devices) if 0 <= i + by < devices]
    return lax.ppermute(array, axis, pairs)


def normalize_kernel(widths, masks, strain_ref, *refs):
    mask_ref = refs[0] if masks else None
    lead_ref, trail_ref = refs[masks : masks + 2]
    flats = refs[masks + 2 : -3]
    held, rows, arrived = refs[-3:]
    samples = strain_ref.shape[0]
    offsets = [sum(widths[:c]) for c in range(len(widths))]
    copies = [
        pltpu.make_async_copy(
            strain_ref.at[:, pl.ds(offset, width)],
            held.at[:, pl.ds(offset, width)],
            arrived.at[c],
        )
        for c, (offset, width) in enumerate(zip(offsets, widths))
    ]
    for copy in copies:
        copy.start()
    row = lax.broadcasted_iota(jnp.int32, (TILE, TILE + SPAN), 0)
    col = lax.broadcasted_iota(jnp.int32, (TILE, TILE + SPAN), 1)
    band = jnp.where((col >= row) & (col <= row + SPAN), 1.0, 0.0).astype(jnp.bfloat16)
    for copy, flat_ref, offset, width in zip(copies, flats, offsets, widths):
        columns = slice(offset, offset + width)
        copy.wait()
        center = held[:, columns]
        if masks:
            alive = jnp.broadcast_to(mask_ref[:, columns] > 0, center.shape)
            center = jnp.where(alive, center.astype(jnp.float32), 0.0).astype(jnp.bfloat16)
        rows[:HALF, :width] = lead_ref[:, columns]
        rows[HALF : HALF + samples, :width] = center
        rows[HALF + samples :, :width] = trail_ref[:, columns]
        out_rows = flat_ref.shape[0]
        for start in range(0, out_rows, TILE):
            count = min(TILE, out_rows - start)
            near = rows[start : start + count + SPAN, :width]
            sums = jnp.dot(
                band[:count, : count + SPAN], jnp.abs(near), preferred_element_type=jnp.float32
            )
            middle = rows[start + HALF : start + HALF + count, :width].astype(jnp.float32)
            flat_ref[start : start + count] = (
                middle / (sums / (2 * HALF + 1) + EPSILON)
            ).astype(jnp.bfloat16)


def params():
    return pltpu.CompilerParams(vmem_limit_bytes=VMEM_BYTES)


def normalize_chunks(strain, mask, lead, trail, widths):
    samples, channels = strain.shape
    masks = [] if mask is None else [mask]
    whole = pl.BlockSpec(memory_space=pltpu.VMEM)
    shapes = [(samples + HALF, width) for width in widths]
    return pl.pallas_call(
        functools.partial(normalize_kernel, widths, len(masks)),
        out_shape=[jax.ShapeDtypeStruct(shape, jnp.bfloat16) for shape in shapes],
        in_specs=[pl.BlockSpec(memory_space=pltpu.HBM)] + [whole] * (len(masks) + 2),
        out_specs=[whole] * len(widths),
        scratch_shapes=[
            pltpu.VMEM((samples, channels), jnp.bfloat16),
            pltpu.VMEM((samples + HALF + SPAN, max(widths)), jnp.bfloat16),
            pltpu.SemaphoreType.DMA((len(widths),)),
        ],
        compiler_params=pltpu.CompilerParams(vmem_limit_bytes=NORMALIZE_BYTES),
        cost_estimate=pl.CostEstimate(
            flops=2 * (samples + HALF) * (TILE + SPAN) * channels,
            bytes_accessed=4 * samples * channels,
            transcendentals=0,
        ),
        name="normalize",
    )(strain, *masks, lead, trail)


def select_kernel(own, me_ref, index_ref, *refs):
    flats, (theirs_ref, mine_ref) = refs[:-2], refs[-2:]
    half = theirs_ref.shape[0]
    me = me_ref[0]
    spot, side = me >> 1, me & 1
    line = half // own
    index = jnp.concatenate(
        [
            index_ref[pl.ds(pl.multiple_of(block * own, own), own), :]
            for far in (1, 0)
            for block in [
                2 * ((spot + by) & (line - 1)) + (side ^ far) for by in range(line)
            ]
        ],
        axis=0,
    )
    offset = me * sum(flat.shape[1] for flat in flats)
    total = jnp.zeros((2 * half, theirs_ref.shape[1]), jnp.float32)
    for flat_ref in flats:
        width = flat_ref.shape[1]
        channel = lax.broadcasted_iota(jnp.int32, (2 * half, width), 1) + offset
        onehot = jnp.where(index == channel, 1.0, 0.0).astype(jnp.bfloat16)
        total += lax.dot_general(
            onehot, flat_ref[...], (((1,), (1,)), ((), ())), preferred_element_type=jnp.float32
        )
        offset += width
    theirs_ref[...] = total[:half].astype(jnp.bfloat16)
    mine_ref[...] = total[half:].astype(jnp.bfloat16)


def select_sources(flats, index, me, samples, own):
    sources = index.shape[0]
    channels = sum(f.shape[1] for f in flats)
    return pl.pallas_call(
        functools.partial(select_kernel, own),
        out_shape=[jax.ShapeDtypeStruct((sources // 2, samples), jnp.bfloat16)] * 2,
        grid_spec=pltpu.PrefetchScalarGridSpec(
            num_scalar_prefetch=1,
            grid=(samples // 256,),
            in_specs=[pl.BlockSpec((sources, 1), lambda i, me: (0, 0))]
            + [pl.BlockSpec((256, f.shape[1]), lambda i, me: (i, 0)) for f in flats],
            out_specs=[pl.BlockSpec((sources // 2, 256), lambda i, me: (0, i))] * 2,
        ),
        compiler_params=params(),
        cost_estimate=pl.CostEstimate(
            flops=2 * sources * samples * channels,
            bytes_accessed=2 * samples * channels,
            transcendentals=0,
        ),
        name="select",
    )(me, index[:, None], *flats)


def hankel_kernel(trace_ref, out_ref):
    width = out_ref.shape[1]
    for source in range(trace_ref.shape[0]):
        spread = jnp.broadcast_to(trace_ref[source : source + 1], (LAGS, width))
        shifted = pltpu.roll(spread, 0, 1, stride=1, stride_axis=0)
        out_ref[source * LAGS : (source + 1) * LAGS] = shifted.astype(jnp.bfloat16)


def hankel(traces):
    sources, samples = traces.shape
    width = samples + 128
    padded = jnp.pad(traces.astype(jnp.float32), ((0, 0), (0, 128)))
    return pl.pallas_call(
        hankel_kernel,
        out_shape=jax.ShapeDtypeStruct((sources * LAGS, width), jnp.bfloat16),
        grid=(sources // 8,),
        in_specs=[pl.BlockSpec((8, width), lambda i: (i, 0))],
        out_specs=pl.BlockSpec((8 * LAGS, width), lambda i: (i, 0)),
        compiler_params=params(),
        cost_estimate=pl.CostEstimate(
            flops=sources * LAGS * width, bytes_accessed=2 * sources * LAGS * width, transcendentals=0
        ),
        name="hankel",
    )(padded)


def at_end(spot):
    return (spot == 0) | (spot == 3)


def origin(slot, me):
    spot, side = me >> 1, me & 1
    near = spot < 2
    there = [
        spot,
        spot ^ 1,
        jnp.where(near, 2, 1),
        jnp.where(near, 3, 0),
    ][slot]
    return 2 * there + side


def correlate_kernel(rows, two, aliased, scale, me_ref, *refs):
    refs = list(refs)
    hankels = [refs.pop(0) for _ in range(rows)]
    first = refs.pop(0)
    second = refs.pop(0) if two else None
    if aliased:
        refs.pop(0)
    held = refs.pop()
    out_ref = refs.pop(0)
    depth, width = first.shape
    step = pl.program_id(0)
    each = hankels[0].shape[0] // ROWS

    @pl.when(step == 0)
    def _():
        held[depth:] = jnp.zeros((held.shape[0] - depth, width), held.dtype)
        if two:
            end = at_end(me_ref[0] >> 1)

            @pl.when(end)
            def _():
                pltpu.sync_copy(first, held.at[pl.ds(0, depth)])

            @pl.when(jnp.logical_not(end))
            def _():
                pltpu.sync_copy(second, held.at[pl.ds(0, depth)])
        else:
            pltpu.sync_copy(first, held.at[pl.ds(0, depth)])

    def product(ref, at):
        lagged = ref[pl.ds(pl.multiple_of(at * ROWS, ROWS), ROWS), :]
        return jnp.dot(lagged, held[...], preferred_element_type=jnp.float32) * scale

    if rows == 1:
        out_ref[...] = product(hankels[0], step).reshape(out_ref.shape).astype(out_ref.dtype)
        return
    sent_ref = refs.pop(0)

    @pl.when(step < each)
    def _():
        sent_ref[...] = product(hankels[1], step).reshape(sent_ref.shape).astype(sent_ref.dtype)

    @pl.when(step >= each)
    def _():
        out_ref[...] = product(hankels[0], step - each).reshape(out_ref.shape)


def correlate(hankels, operands, me, place, scale, out, channels, sent=False):
    lanes, span = hankels[0].shape
    sources = lanes // LAGS
    depth, width = operands[0].shape
    group = ROWS // LAGS
    each = lanes // ROWS
    rows = len(hankels)
    skip = (rows - 1) * each
    resident = pl.BlockSpec(memory_space=pltpu.VMEM)
    in_specs = [resident] * rows
    in_specs += [pl.BlockSpec(memory_space=pl.ANY)] * len(operands)
    arguments = [*hankels, *operands]
    aliases = {}
    if out is not None and not sent:
        in_specs.append(pl.BlockSpec(memory_space=pl.ANY))
        arguments.append(out)
        aliases = {len(arguments): 0}
    sent_shape = jax.ShapeDtypeStruct((sources, LAGS, width), jnp.bfloat16)
    sent_spec = pl.BlockSpec((group, LAGS, width), lambda i, me: (jnp.minimum(i, each - 1), 0, 0))
    out_shape = [jax.ShapeDtypeStruct((1, sources, LAGS, channels), jnp.float32)]
    out_specs = [
        pl.BlockSpec(
            (pl.Element(1), pl.Element(group), pl.Element(LAGS), pl.Element(width)),
            lambda i, me: (
                0,
                jnp.maximum(i - skip, 0) * group,
                0,
                pl.multiple_of(place(me[0]), 128),
            ),
        )
    ]
    if rows == 2:
        out_shape.append(sent_shape)
        out_specs.append(sent_spec)
    if sent:
        out_shape, out_specs = [sent_shape], [sent_spec]
    return pl.pallas_call(
        functools.partial(correlate_kernel, rows, len(operands) == 2, bool(aliases), scale),
        out_shape=out_shape,
        grid_spec=pltpu.PrefetchScalarGridSpec(
            num_scalar_prefetch=1,
            grid=(rows * each,),
            in_specs=in_specs,
            out_specs=out_specs,
            scratch_shapes=[pltpu.VMEM((span, width), jnp.bfloat16)],
        ),
        input_output_aliases=aliases,
        compiler_params=params(),
        cost_estimate=pl.CostEstimate(
            flops=2 * rows * lanes * span * width,
            bytes_accessed=2 * depth * width + 4 * lanes * width,
            transcendentals=0,
        ),
        name="correlate",
    )(me, *arguments)


def store_kernel(me_ref, got_ref, kept_ref, out_ref):
    out_ref[...] = got_ref[...].astype(jnp.float32)[None]


def store(got, me, place, out):
    sources, lags, width = got.shape
    group = ROWS // LAGS
    return pl.pallas_call(
        store_kernel,
        out_shape=jax.ShapeDtypeStruct(out.shape, out.dtype),
        grid_spec=pltpu.PrefetchScalarGridSpec(
            num_scalar_prefetch=1,
            grid=(sources // group,),
            in_specs=[
                pl.BlockSpec((group, lags, width), lambda i, me: (i, 0, 0)),
                pl.BlockSpec(memory_space=pl.ANY),
            ],
            out_specs=pl.BlockSpec(
                (pl.Element(1), pl.Element(group), pl.Element(lags), pl.Element(width)),
                lambda i, me: (0, i * group, 0, pl.multiple_of(place(me[0]), 128)),
            ),
        ),
        input_output_aliases={2: 0},
        compiler_params=params(),
        cost_estimate=pl.CostEstimate(
            flops=0, bytes_accessed=6 * sources * lags * width, transcendentals=0
        ),
        name="store",
    )(me, got, out)


def hop(array, pairs):
    return lax.ppermute(array, "src", pairs)


def line_of_four(strain, dead_mask, src_index):
    samples, channels = strain.shape
    devices = lax.axis_size("src")
    line = devices // 2
    count = len(WIDTHS)
    offsets = [sum(WIDTHS[:c]) for c in range(count)]
    total = channels * devices
    own = src_index.shape[0] // devices
    scale = 1.0 / math.sqrt(samples)
    me = lax.axis_index("src")

    def along(pairs):
        return [(2 * a + s, 2 * b + s) for a, b in pairs for s in range(2)]

    outer = along([(0, 1), (1, 0), (2, 3), (3, 2)])
    inner = along([(1, 2), (2, 1)])
    outward = along([(1, 0), (2, 3)])
    across = [(i, i ^ 1) for i in range(devices)]

    def masked(rows):
        return jnp.where(dead_mask > 0, rows, jnp.zeros((), rows.dtype))

    def around(rows):
        trail = passed_along(rows(0, SPAN), "win", -1)
        lead = passed_along(rows(samples - HALF, samples), "win", 1)
        return lead, trail

    raw = jnp.where(
        dead_mask[:, : WIDTHS[0]] > 0, strain[:, : WIDTHS[0]], jnp.zeros((), strain.dtype)
    )
    raw_out = hop(raw, outer)
    raw_in = hop(raw, inner)
    lead, trail = around(lambda a, b: masked(strain[a:b]))
    alive = (dead_mask > 0).astype(jnp.int32)
    flats = normalize_chunks(strain, alive, lead, trail, WIDTHS)

    here = jnp.reshape(me, (1,)).astype(jnp.int32)
    theirs, mine = select_sources(flats, src_index, here, samples, own)
    heard = hop(theirs, across)
    blocks = [
        mine[by * own : (by + 1) * own] + heard[by * own : (by + 1) * own] for by in range(line)
    ]
    traces = blocks[0]
    for by in range(1, line):
        traces = traces + hop(blocks[by], along([(i, (i + by) % line) for i in range(line)]))
    partner_traces = hop(traces, across)
    own_rows = hankel(traces)
    partner_rows = hankel(partner_traces)

    def hops(arrays, pairs):
        return [hop(a, pairs) for a in arrays]

    def received(chunk):
        before, after = around(lambda a, b: chunk[a:b])
        (flat,) = normalize_chunks(chunk, None, before, after, WIDTHS[:1])
        return flat

    first_out = [received(raw_out)]
    first_in = [received(raw_in)]
    first_out += [hop(flats[c], outer) for c in range(1, count)]
    first_in += [hop(flats[c], inner) for c in range(1, count)]
    swapped = hop(flats[SHARED], across)
    second_out = hops(first_in, outward)
    second_in = hops(first_out, inner)
    third_out = hops(second_in, outward)

    arrivals = [
        [[f] for f in flats],
        [[f] for f in first_out],
        [list(pair) for pair in zip(second_out, first_in)],
        [list(pair) for pair in zip(third_out, second_in)],
    ]
    out = None
    waiting = []

    def place(slot, c, partner):
        return lambda me: (origin(slot, me) ^ partner) * channels + offsets[c]

    def add(slot, c, partner, chunk, hankels):
        nonlocal out
        out, *sent = correlate(
            hankels, chunk, here, place(slot, c, partner), scale, out, total
        )
        return sent

    def keep():
        nonlocal out
        out = store(*waiting.pop(0), out)

    add(0, SHARED, 0, [flats[SHARED]], [own_rows])
    for slot, c in STEPS:
        chunk = arrivals[slot][c]
        if slot < line - 1:
            (made,) = add(slot, c, 0, chunk, [own_rows, partner_rows])
        else:
            (made,) = correlate(
                [partner_rows], chunk, here, place(slot, c, 0), scale, out, total, sent=True
            )
            add(slot, c, 0, chunk, [own_rows])
        waiting.append((hop(made, across), here, place(slot, c, 1)))
        if (slot, c) == (0, count - 1):
            add(0, SHARED, 1, [swapped], [own_rows])
        for _ in range(STORED.get((slot, c), 0)):
            keep()
    while waiting:
        keep()
    return out


def gathered(strain, dead_mask, src_index):
    samples, channels = strain.shape
    devices = lax.axis_size("src")
    scale = 1.0 / math.sqrt(samples)
    masked = jnp.where(dead_mask > 0, strain, jnp.zeros((), strain.dtype))
    lead = passed_along(masked[samples - HALF :], "win", 1)
    trail = passed_along(masked[:SPAN], "win", -1)
    rows = jnp.concatenate([lead, masked, trail], axis=0).astype(jnp.float32)
    sums = lax.reduce_window(
        jnp.abs(rows), jnp.zeros((), jnp.float32), lax.add, (2 * HALF + 1, 1), (1, 1), "VALID"
    )
    center = rows[HALF : rows.shape[0] - HALF]
    flat = (center / (sums / (2 * HALF + 1) + EPSILON)).astype(jnp.bfloat16)
    offset = lax.axis_index("src") * channels
    onehot = (src_index[:, None] - offset == jnp.arange(channels, dtype=jnp.int32)[None, :]).astype(
        jnp.bfloat16
    )
    selected = lax.dot_general(
        onehot, flat[:samples], (((1,), (1,)), ((), ())), preferred_element_type=jnp.float32
    )
    traces = lax.psum_scatter(
        selected.astype(jnp.bfloat16), "src", scatter_dimension=0, tiled=True
    )
    sources = traces.shape[0]
    tail = flat.shape[0] - samples
    shifted = [jnp.pad(traces, ((0, 0), (lag, tail - lag))) for lag in range(LAGS)]
    lagged = jnp.stack(shifted, axis=1).reshape(sources * LAGS, flat.shape[0])
    everywhere = lax.all_gather(flat, "src", axis=1, tiled=True)
    joined = jnp.dot(lagged, everywhere, preferred_element_type=jnp.float32) * scale
    return joined.reshape(1, sources, LAGS, channels * devices)


def lined(devices, channels):
    return devices == 8 and channels == sum(WIDTHS)


def shards(strain, dead_mask, src_index):
    if lined(lax.axis_size("src"), strain.shape[1]):
        return line_of_four(strain, dead_mask, src_index)
    return gathered(strain, dead_mask, src_index)


def solution(mesh):
    in_specs = (P("win", "src"), P("win", "src"), P())
    out_specs = P("win", "src", None, None)
    return jax.shard_map(shards, mesh=mesh, in_specs=in_specs, out_specs=out_specs, check_vma=False)
```

```python
import functools
import math

import jax
import jax.numpy as jnp
from jax import lax
from jax.experimental import pallas as pl
from jax.experimental.pallas import tpu as pltpu
from jax.sharding import PartitionSpec as P


LAGS = 32
HALF = 32
EPSILON = 1e-05
TILE = 192
SPAN = 2 * HALF
ROWS = 512
VMEM_BYTES = 24 << 20
NORMALIZE_BYTES = 50 << 20

WIDTHS = (384, 384, 256, 128, 128)
EARLY = (0, 1, 2, 3, 4)
LATE = (0, 1, 2, 3, 4)
SHARED = 2
STEPS = (
    [(0, c) for c in LATE if c != SHARED]
    + [(1, c) for c in EARLY]
    + [(2, c) for c in LATE]
    + [(3, c) for c in LATE]
)
STORED = {(1, 4): 5, (2, 0): 3, (2, 1): 1, (2, 2): 1, (2, 4): 3, (3, 0): 2, (3, 3): 1}


def passed_along(array, axis, by):
    devices = lax.axis_size(axis)
    pairs = [(i, i + by) for i in range(devices) if 0 <= i + by < devices]
    return lax.ppermute(array, axis, pairs)


def normalize_kernel(widths, masks, strain_ref, *refs):
    mask_ref = refs[0] if masks else None
    lead_ref, trail_ref = refs[masks : masks + 2]
    flats = refs[masks + 2 : -3]
    held, rows, arrived = refs[-3:]
    samples = strain_ref.shape[0]
    offsets = [sum(widths[:c]) for c in range(len(widths))]
    copies = [
        pltpu.make_async_copy(
            strain_ref.at[:, pl.ds(offset, width)],
            held.at[:, pl.ds(offset, width)],
            arrived.at[c],
        )
        for c, (offset, width) in enumerate(zip(offsets, widths))
    ]
    for copy in copies:
        copy.start()
    row = lax.broadcasted_iota(jnp.int32, (TILE, TILE + SPAN), 0)
    col = lax.broadcasted_iota(jnp.int32, (TILE, TILE + SPAN), 1)
    band = jnp.where((col >= row) & (col <= row + SPAN), 1.0, 0.0).astype(jnp.bfloat16)
    for copy, flat_ref, offset, width in zip(copies, flats, offsets, widths):
        columns = slice(offset, offset + width)
        copy.wait()
        center = held[:, columns]
        if masks:
            alive = jnp.broadcast_to(mask_ref[:, columns] > 0, center.shape)
            center = jnp.where(alive, center.astype(jnp.float32), 0.0).astype(jnp.bfloat16)
        rows[:HALF, :width] = lead_ref[:, columns]
        rows[HALF : HALF + samples, :width] = center
        rows[HALF + samples :, :width] = trail_ref[:, columns]
        out_rows = flat_ref.shape[0]
        for start in range(0, out_rows, TILE):
            count = min(TILE, out_rows - start)
            near = rows[start : start + count + SPAN, :width]
            sums = jnp.dot(
                band[:count, : count + SPAN], jnp.abs(near), preferred_element_type=jnp.float32
            )
            middle = rows[start + HALF : start + HALF + count, :width].astype(jnp.float32)
            flat_ref[start : start + count] = (
                middle / (sums / (2 * HALF + 1) + EPSILON)
            ).astype(jnp.bfloat16)


def params():
    return pltpu.CompilerParams(vmem_limit_bytes=VMEM_BYTES)


def normalize_chunks(strain, mask, lead, trail, widths):
    samples, channels = strain.shape
    masks = [] if mask is None else [mask]
    whole = pl.BlockSpec(memory_space=pltpu.VMEM)
    shapes = [(samples + HALF, width) for width in widths]
    return pl.pallas_call(
        functools.partial(normalize_kernel, widths, len(masks)),
        out_shape=[jax.ShapeDtypeStruct(shape, jnp.bfloat16) for shape in shapes],
        in_specs=[pl.BlockSpec(memory_space=pltpu.HBM)] + [whole] * (len(masks) + 2),
        out_specs=[whole] * len(widths),
        scratch_shapes=[
            pltpu.VMEM((samples, channels), jnp.bfloat16),
            pltpu.VMEM((samples + HALF + SPAN, max(widths)), jnp.bfloat16),
            pltpu.SemaphoreType.DMA((len(widths),)),
        ],
        compiler_params=pltpu.CompilerParams(vmem_limit_bytes=NORMALIZE_BYTES),
        cost_estimate=pl.CostEstimate(
            flops=2 * (samples + HALF) * (TILE + SPAN) * channels,
            bytes_accessed=4 * samples * channels,
            transcendentals=0,
        ),
        name="normalize",
    )(strain, *masks, lead, trail)


def select_kernel(own, me_ref, index_ref, *refs):
    flats, (theirs_ref, mine_ref) = refs[:-2], refs[-2:]
    half = theirs_ref.shape[0]
    me = me_ref[0]
    spot, side = me >> 1, me & 1
    line = half // own
    index = jnp.concatenate(
        [
            index_ref[pl.ds(pl.multiple_of(block * own, own), own), :]
            for far in (1, 0)
            for block in [
                2 * ((spot + by) & (line - 1)) + (side ^ far) for by in range(line)
            ]
        ],
        axis=0,
    )
    offset = me * sum(flat.shape[1] for flat in flats)
    total = jnp.zeros((2 * half, theirs_ref.shape[1]), jnp.float32)
    for flat_ref in flats:
        width = flat_ref.shape[1]
        channel = lax.broadcasted_iota(jnp.int32, (2 * half, width), 1) + offset
        onehot = jnp.where(index == channel, 1.0, 0.0).astype(jnp.bfloat16)
        total += lax.dot_general(
            onehot, flat_ref[...], (((1,), (1,)), ((), ())), preferred_element_type=jnp.float32
        )
        offset += width
    theirs_ref[...] = total[:half].astype(jnp.bfloat16)
    mine_ref[...] = total[half:].astype(jnp.bfloat16)


def select_sources(flats, index, me, samples, own):
    sources = index.shape[0]
    channels = sum(f.shape[1] for f in flats)
    return pl.pallas_call(
        functools.partial(select_kernel, own),
        out_shape=[jax.ShapeDtypeStruct((sources // 2, samples), jnp.bfloat16)] * 2,
        grid_spec=pltpu.PrefetchScalarGridSpec(
            num_scalar_prefetch=1,
            grid=(samples // 256,),
            in_specs=[pl.BlockSpec((sources, 1), lambda i, me: (0, 0))]
            + [pl.BlockSpec((256, f.shape[1]), lambda i, me: (i, 0)) for f in flats],
            out_specs=[pl.BlockSpec((sources // 2, 256), lambda i, me: (0, i))] * 2,
        ),
        compiler_params=params(),
        cost_estimate=pl.CostEstimate(
            flops=2 * sources * samples * channels,
            bytes_accessed=2 * samples * channels,
            transcendentals=0,
        ),
        name="select",
    )(me, index[:, None], *flats)


def hankel_kernel(trace_ref, out_ref):
    width = out_ref.shape[1]
    for source in range(trace_ref.shape[0]):
        spread = jnp.broadcast_to(trace_ref[source : source + 1], (LAGS, width))
        shifted = pltpu.roll(spread, 0, 1, stride=1, stride_axis=0)
        out_ref[source * LAGS : (source + 1) * LAGS] = shifted.astype(jnp.bfloat16)


def hankel(traces):
    sources, samples = traces.shape
    width = samples + 128
    padded = jnp.pad(traces.astype(jnp.float32), ((0, 0), (0, 128)))
    return pl.pallas_call(
        hankel_kernel,
        out_shape=jax.ShapeDtypeStruct((sources * LAGS, width), jnp.bfloat16),
        grid=(sources // 8,),
        in_specs=[pl.BlockSpec((8, width), lambda i: (i, 0))],
        out_specs=pl.BlockSpec((8 * LAGS, width), lambda i: (i, 0)),
        compiler_params=params(),
        cost_estimate=pl.CostEstimate(
            flops=sources * LAGS * width, bytes_accessed=2 * sources * LAGS * width, transcendentals=0
        ),
        name="hankel",
    )(padded)


def at_end(spot):
    return (spot == 0) | (spot == 3)


def origin(slot, me):
    spot, side = me >> 1, me & 1
    near = spot < 2
    there = [
        spot,
        spot ^ 1,
        jnp.where(near, 2, 1),
        jnp.where(near, 3, 0),
    ][slot]
    return 2 * there + side


def correlate_kernel(tile, rows, two, aliased, scale, me_ref, *refs):
    refs = list(refs)
    hankels = [refs.pop(0) for _ in range(rows)]
    first = refs.pop(0)
    second = refs.pop(0) if two else None
    if aliased:
        refs.pop(0)
    held = refs.pop()
    out_ref = refs.pop(0)
    depth, width = first.shape
    step = pl.program_id(0)
    each = hankels[0].shape[0] // tile

    @pl.when(step == 0)
    def _():
        held[depth:] = jnp.zeros((held.shape[0] - depth, width), held.dtype)
        if two:
            end = at_end(me_ref[0] >> 1)

            @pl.when(end)
            def _():
                pltpu.sync_copy(first, held.at[pl.ds(0, depth)])

            @pl.when(jnp.logical_not(end))
            def _():
                pltpu.sync_copy(second, held.at[pl.ds(0, depth)])
        else:
            pltpu.sync_copy(first, held.at[pl.ds(0, depth)])

    def product(ref, at):
        lagged = ref[pl.ds(pl.multiple_of(at * tile, tile), tile), :]
        return jnp.dot(lagged, held[...], preferred_element_type=jnp.float32) * scale

    if rows == 1:
        out_ref[...] = product(hankels[0], step).reshape(out_ref.shape).astype(out_ref.dtype)
        return
    sent_ref = refs.pop(0)

    @pl.when(step < each)
    def _():
        sent_ref[...] = product(hankels[1], step).reshape(sent_ref.shape).astype(sent_ref.dtype)

    @pl.when(step >= each)
    def _():
        out_ref[...] = product(hankels[0], step - each).reshape(out_ref.shape)


def correlate(hankels, operands, me, place, scale, out, channels, tile, sent=False):
    lanes, span = hankels[0].shape
    sources = lanes // LAGS
    depth, width = operands[0].shape
    group = tile // LAGS
    each = lanes // tile
    rows = len(hankels)
    skip = (rows - 1) * each
    resident = pl.BlockSpec(memory_space=pltpu.VMEM)
    in_specs = [resident] * rows
    in_specs += [pl.BlockSpec(memory_space=pl.ANY)] * len(operands)
    arguments = [*hankels, *operands]
    aliases = {}
    if out is not None and not sent:
        in_specs.append(pl.BlockSpec(memory_space=pl.ANY))
        arguments.append(out)
        aliases = {len(arguments): 0}
    sent_shape = jax.ShapeDtypeStruct((sources, LAGS, width), jnp.bfloat16)
    sent_spec = pl.BlockSpec((group, LAGS, width), lambda i, me: (jnp.minimum(i, each - 1), 0, 0))
    out_shape = [jax.ShapeDtypeStruct((1, sources, LAGS, channels), jnp.float32)]
    out_specs = [
        pl.BlockSpec(
            (pl.Element(1), pl.Element(group), pl.Element(LAGS), pl.Element(width)),
            lambda i, me: (
                0,
                jnp.maximum(i - skip, 0) * group,
                0,
                pl.multiple_of(place(me[0]), 128),
            ),
        )
    ]
    if rows == 2:
        out_shape.append(sent_shape)
        out_specs.append(sent_spec)
    if sent:
        out_shape, out_specs = [sent_shape], [sent_spec]
    return pl.pallas_call(
        functools.partial(correlate_kernel, tile, rows, len(operands) == 2, bool(aliases), scale),
        out_shape=out_shape,
        grid_spec=pltpu.PrefetchScalarGridSpec(
            num_scalar_prefetch=1,
            grid=(rows * each,),
            in_specs=in_specs,
            out_specs=out_specs,
            scratch_shapes=[pltpu.VMEM((span, width), jnp.bfloat16)],
        ),
        input_output_aliases=aliases,
        compiler_params=params(),
        cost_estimate=pl.CostEstimate(
            flops=2 * rows * lanes * span * width,
            bytes_accessed=2 * depth * width + 4 * lanes * width,
            transcendentals=0,
        ),
        name="correlate",
    )(me, *arguments)


def store_kernel(me_ref, got_ref, kept_ref, out_ref):
    out_ref[...] = got_ref[...].astype(jnp.float32)[None]


def store(got, me, place, out):
    sources, lags, width = got.shape
    group = ROWS // LAGS
    return pl.pallas_call(
        store_kernel,
        out_shape=jax.ShapeDtypeStruct(out.shape, out.dtype),
        grid_spec=pltpu.PrefetchScalarGridSpec(
            num_scalar_prefetch=1,
            grid=(sources // group,),
            in_specs=[
                pl.BlockSpec((group, lags, width), lambda i, me: (i, 0, 0)),
                pl.BlockSpec(memory_space=pl.ANY),
            ],
            out_specs=pl.BlockSpec(
                (pl.Element(1), pl.Element(group), pl.Element(lags), pl.Element(width)),
                lambda i, me: (0, i * group, 0, pl.multiple_of(place(me[0]), 128)),
            ),
        ),
        input_output_aliases={2: 0},
        compiler_params=params(),
        cost_estimate=pl.CostEstimate(
            flops=0, bytes_accessed=6 * sources * lags * width, transcendentals=0
        ),
        name="store",
    )(me, got, out)


def hop(array, pairs):
    return lax.ppermute(array, "src", pairs)


def line_of_four(strain, dead_mask, src_index):
    samples, channels = strain.shape
    devices = lax.axis_size("src")
    line = devices // 2
    count = len(WIDTHS)
    offsets = [sum(WIDTHS[:c]) for c in range(count)]
    total = channels * devices
    own = src_index.shape[0] // devices
    scale = 1.0 / math.sqrt(samples)
    me = lax.axis_index("src")

    def along(pairs):
        return [(2 * a + s, 2 * b + s) for a, b in pairs for s in range(2)]

    outer = along([(0, 1), (1, 0), (2, 3), (3, 2)])
    inner = along([(1, 2), (2, 1)])
    outward = along([(1, 0), (2, 3)])
    across = [(i, i ^ 1) for i in range(devices)]

    def masked(rows):
        return jnp.where(dead_mask > 0, rows, jnp.zeros((), rows.dtype))

    def around(rows):
        trail = passed_along(rows(0, SPAN), "win", -1)
        lead = passed_along(rows(samples - HALF, samples), "win", 1)
        return lead, trail

    raw = jnp.where(
        dead_mask[:, : WIDTHS[0]] > 0, strain[:, : WIDTHS[0]], jnp.zeros((), strain.dtype)
    )
    raw_out = hop(raw, outer)
    raw_in = hop(raw, inner)
    lead, trail = around(lambda a, b: masked(strain[a:b]))
    alive = (dead_mask > 0).astype(jnp.int32)
    flats = normalize_chunks(strain, alive, lead, trail, WIDTHS)

    here = jnp.reshape(me, (1,)).astype(jnp.int32)
    theirs, mine = select_sources(flats, src_index, here, samples, own)
    heard = hop(theirs, across)
    blocks = [
        mine[by * own : (by + 1) * own] + heard[by * own : (by + 1) * own] for by in range(line)
    ]
    traces = blocks[0]
    for by in range(1, line):
        traces = traces + hop(blocks[by], along([(i, (i + by) % line) for i in range(line)]))
    partner_traces = hop(traces, across)
    own_rows = hankel(traces)
    partner_rows = hankel(partner_traces)

    def hops(arrays, pairs):
        return [hop(a, pairs) for a in arrays]

    def received(chunk):
        before, after = around(lambda a, b: chunk[a:b])
        (flat,) = normalize_chunks(chunk, None, before, after, WIDTHS[:1])
        return flat

    first_out = [received(raw_out)]
    first_in = [received(raw_in)]
    first_out += [hop(flats[c], outer) for c in range(1, count)]
    first_in += [hop(flats[c], inner) for c in range(1, count)]
    swapped = hop(flats[SHARED], across)
    second_out = hops(first_in, outward)
    second_in = hops(first_out, inner)
    third_out = hops(second_in, outward)

    arrivals = [
        [[f] for f in flats],
        [[f] for f in first_out],
        [list(pair) for pair in zip(second_out, first_in)],
        [list(pair) for pair in zip(third_out, second_in)],
    ]
    out = None
    waiting = []
    tiles = [ROWS // 2] * (line - 1) + [ROWS]

    def place(slot, c, partner):
        return lambda me: (origin(slot, me) ^ partner) * channels + offsets[c]

    def add(slot, c, partner, chunk, hankels):
        nonlocal out
        out, *sent = correlate(
            hankels, chunk, here, place(slot, c, partner), scale, out, total, tiles[slot]
        )
        return sent

    def keep():
        nonlocal out
        out = store(*waiting.pop(0), out)

    add(0, SHARED, 0, [flats[SHARED]], [own_rows])
    for slot, c in STEPS:
        chunk = arrivals[slot][c]
        if slot < line - 1:
            (made,) = add(slot, c, 0, chunk, [own_rows, partner_rows])
        else:
            (made,) = correlate(
                [partner_rows],
                chunk,
                here,
                place(slot, c, 0),
                scale,
                out,
                total,
                tiles[slot],
                sent=True,
            )
            add(slot, c, 0, chunk, [own_rows])
        waiting.append((hop(made, across), here, place(slot, c, 1)))
        if (slot, c) == (0, count - 1):
            add(0, SHARED, 1, [swapped], [own_rows])
        for _ in range(STORED.get((slot, c), 0)):
            keep()
    while waiting:
        keep()
    return out


def gathered(strain, dead_mask, src_index):
    samples, channels = strain.shape
    devices = lax.axis_size("src")
    scale = 1.0 / math.sqrt(samples)
    masked = jnp.where(dead_mask > 0, strain, jnp.zeros((), strain.dtype))
    lead = passed_along(masked[samples - HALF :], "win", 1)
    trail = passed_along(masked[:SPAN], "win", -1)
    rows = jnp.concatenate([lead, masked, trail], axis=0).astype(jnp.float32)
    sums = lax.reduce_window(
        jnp.abs(rows), jnp.zeros((), jnp.float32), lax.add, (2 * HALF + 1, 1), (1, 1), "VALID"
    )
    center = rows[HALF : rows.shape[0] - HALF]
    flat = (center / (sums / (2 * HALF + 1) + EPSILON)).astype(jnp.bfloat16)
    offset = lax.axis_index("src") * channels
    onehot = (src_index[:, None] - offset == jnp.arange(channels, dtype=jnp.int32)[None, :]).astype(
        jnp.bfloat16
    )
    selected = lax.dot_general(
        onehot, flat[:samples], (((1,), (1,)), ((), ())), preferred_element_type=jnp.float32
    )
    traces = lax.psum_scatter(
        selected.astype(jnp.bfloat16), "src", scatter_dimension=0, tiled=True
    )
    sources = traces.shape[0]
    tail = flat.shape[0] - samples
    shifted = [jnp.pad(traces, ((0, 0), (lag, tail - lag))) for lag in range(LAGS)]
    lagged = jnp.stack(shifted, axis=1).reshape(sources * LAGS, flat.shape[0])
    everywhere = lax.all_gather(flat, "src", axis=1, tiled=True)
    joined = jnp.dot(lagged, everywhere, preferred_element_type=jnp.float32) * scale
    return joined.reshape(1, sources, LAGS, channels * devices)


def lined(devices, channels):
    return devices == 8 and channels == sum(WIDTHS)


def shards(strain, dead_mask, src_index):
    if lined(lax.axis_size("src"), strain.shape[1]):
        return line_of_four(strain, dead_mask, src_index)
    return gathered(strain, dead_mask, src_index)


def solution(mesh):
    in_specs = (P("win", "src"), P("win", "src"), P())
    out_specs = P("win", "src", None, None)
    return jax.shard_map(shards, mesh=mesh, in_specs=in_specs, out_specs=out_specs, check_vma=False)
```

```python
import functools
import math

import jax
import jax.numpy as jnp
from jax import lax
from jax.experimental import pallas as pl
from jax.experimental.pallas import tpu as pltpu
from jax.sharding import PartitionSpec as P


LAGS = 32
HALF = 32
EPSILON = 1e-05
TILE = 192
SPAN = 2 * HALF
ROWS = 512
VMEM_BYTES = 24 << 20
NORMALIZE_BYTES = 50 << 20

WIDTHS = (384, 512, 256, 128)
EARLY = (0, 1, 2, 3)
LATE = (1, 0, 2, 3)
SHARED = 2
STEPS = (
    [(0, c) for c in LATE if c != SHARED]
    + [(1, c) for c in EARLY]
    + [(2, c) for c in LATE]
    + [(3, c) for c in LATE]
)
STORED = {(1, 3): 4, (2, 1): 3, (2, 2): 1, (2, 3): 3, (3, 0): 1}


def passed_along(array, axis, by):
    devices = lax.axis_size(axis)
    pairs = [(i, i + by) for i in range(devices) if 0 <= i + by < devices]
    return lax.ppermute(array, axis, pairs)


def normalize_kernel(widths, masks, strain_ref, *refs):
    mask_ref = refs[0] if masks else None
    lead_ref, trail_ref = refs[masks : masks + 2]
    flats = refs[masks + 2 : -3]
    held, rows, arrived = refs[-3:]
    samples = strain_ref.shape[0]
    offsets = [sum(widths[:c]) for c in range(len(widths))]
    copies = [
        pltpu.make_async_copy(
            strain_ref.at[:, pl.ds(offset, width)],
            held.at[:, pl.ds(offset, width)],
            arrived.at[c],
        )
        for c, (offset, width) in enumerate(zip(offsets, widths))
    ]
    for copy in copies:
        copy.start()
    row = lax.broadcasted_iota(jnp.int32, (TILE, TILE + SPAN), 0)
    col = lax.broadcasted_iota(jnp.int32, (TILE, TILE + SPAN), 1)
    band = jnp.where((col >= row) & (col <= row + SPAN), 1.0, 0.0).astype(jnp.bfloat16)
    for copy, flat_ref, offset, width in zip(copies, flats, offsets, widths):
        columns = slice(offset, offset + width)
        copy.wait()
        center = held[:, columns]
        if masks:
            alive = jnp.broadcast_to(mask_ref[:, columns] > 0, center.shape)
            center = jnp.where(alive, center.astype(jnp.float32), 0.0).astype(jnp.bfloat16)
        rows[:HALF, :width] = lead_ref[:, columns]
        rows[HALF : HALF + samples, :width] = center
        rows[HALF + samples :, :width] = trail_ref[:, columns]
        out_rows = flat_ref.shape[0]
        for start in range(0, out_rows, TILE):
            count = min(TILE, out_rows - start)
            near = rows[start : start + count + SPAN, :width]
            sums = jnp.dot(
                band[:count, : count + SPAN], jnp.abs(near), preferred_element_type=jnp.float32
            )
            middle = rows[start + HALF : start + HALF + count, :width].astype(jnp.float32)
            flat_ref[start : start + count] = (
                middle / (sums / (2 * HALF + 1) + EPSILON)
            ).astype(jnp.bfloat16)


def params():
    return pltpu.CompilerParams(vmem_limit_bytes=VMEM_BYTES)


def normalize_chunks(strain, mask, lead, trail, widths):
    samples, channels = strain.shape
    masks = [] if mask is None else [mask]
    whole = pl.BlockSpec(memory_space=pltpu.VMEM)
    shapes = [(samples + HALF, width) for width in widths]
    return pl.pallas_call(
        functools.partial(normalize_kernel, widths, len(masks)),
        out_shape=[jax.ShapeDtypeStruct(shape, jnp.bfloat16) for shape in shapes],
        in_specs=[pl.BlockSpec(memory_space=pltpu.HBM)] + [whole] * (len(masks) + 2),
        out_specs=[whole] * len(widths),
        scratch_shapes=[
            pltpu.VMEM((samples, channels), jnp.bfloat16),
            pltpu.VMEM((samples + HALF + SPAN, max(widths)), jnp.bfloat16),
            pltpu.SemaphoreType.DMA((len(widths),)),
        ],
        compiler_params=pltpu.CompilerParams(vmem_limit_bytes=NORMALIZE_BYTES),
        cost_estimate=pl.CostEstimate(
            flops=2 * (samples + HALF) * (TILE + SPAN) * channels,
            bytes_accessed=4 * samples * channels,
            transcendentals=0,
        ),
        name="normalize",
    )(strain, *masks, lead, trail)


def mask_kernel(strain_ref, mask_ref, out_ref, held, alive, arrived):
    columns = pl.ds(0, out_ref.shape[1])
    copies = [
        pltpu.make_async_copy(strain_ref.at[:, columns], held, arrived.at[0]),
        pltpu.make_async_copy(mask_ref.at[:, columns], alive, arrived.at[1]),
    ]
    for copy in copies:
        copy.start()
    for copy in copies:
        copy.wait()
    keep = jnp.broadcast_to(alive[...] > 0, held.shape)
    out_ref[...] = jnp.where(keep, held[...].astype(jnp.float32), 0.0).astype(jnp.bfloat16)


def mask_first(strain, mask, width):
    samples = strain.shape[0]
    return pl.pallas_call(
        mask_kernel,
        out_shape=jax.ShapeDtypeStruct((samples, width), jnp.bfloat16),
        in_specs=[pl.BlockSpec(memory_space=pltpu.HBM)] * 2,
        out_specs=pl.BlockSpec(memory_space=pltpu.VMEM),
        scratch_shapes=[
            pltpu.VMEM((samples, width), jnp.bfloat16),
            pltpu.VMEM((1, width), jnp.int32),
            pltpu.SemaphoreType.DMA((2,)),
        ],
        compiler_params=pltpu.CompilerParams(vmem_limit_bytes=NORMALIZE_BYTES),
        cost_estimate=pl.CostEstimate(
            flops=samples * width, bytes_accessed=4 * samples * width, transcendentals=0
        ),
        name="mask",
    )(strain, mask)


def select_kernel(own, me_ref, index_ref, *refs):
    flats, (theirs_ref, mine_ref) = refs[:-2], refs[-2:]
    half = theirs_ref.shape[0]
    me = me_ref[0]
    spot, side = me >> 1, me & 1
    line = half // own
    index = jnp.concatenate(
        [
            index_ref[pl.ds(pl.multiple_of(block * own, own), own), :]
            for far in (1, 0)
            for block in [
                2 * ((spot + by) & (line - 1)) + (side ^ far) for by in range(line)
            ]
        ],
        axis=0,
    )
    offset = me * sum(flat.shape[1] for flat in flats)
    total = jnp.zeros((2 * half, theirs_ref.shape[1]), jnp.float32)
    for flat_ref in flats:
        width = flat_ref.shape[1]
        channel = lax.broadcasted_iota(jnp.int32, (2 * half, width), 1) + offset
        onehot = jnp.where(index == channel, 1.0, 0.0).astype(jnp.bfloat16)
        total += lax.dot_general(
            onehot, flat_ref[...], (((1,), (1,)), ((), ())), preferred_element_type=jnp.float32
        )
        offset += width
    theirs_ref[...] = total[:half].astype(jnp.bfloat16)
    mine_ref[...] = total[half:].astype(jnp.bfloat16)


def select_sources(flats, index, me, samples, own):
    sources = index.shape[0]
    channels = sum(f.shape[1] for f in flats)
    return pl.pallas_call(
        functools.partial(select_kernel, own),
        out_shape=[jax.ShapeDtypeStruct((sources // 2, samples), jnp.bfloat16)] * 2,
        grid_spec=pltpu.PrefetchScalarGridSpec(
            num_scalar_prefetch=1,
            grid=(samples // 256,),
            in_specs=[pl.BlockSpec((sources, 1), lambda i, me: (0, 0))]
            + [pl.BlockSpec((256, f.shape[1]), lambda i, me: (i, 0)) for f in flats],
            out_specs=[pl.BlockSpec((sources // 2, 256), lambda i, me: (0, i))] * 2,
        ),
        compiler_params=params(),
        cost_estimate=pl.CostEstimate(
            flops=2 * sources * samples * channels,
            bytes_accessed=2 * samples * channels,
            transcendentals=0,
        ),
        name="select",
    )(me, index[:, None], *flats)


def hankel_kernel(trace_ref, out_ref):
    width = out_ref.shape[1]
    for source in range(trace_ref.shape[0]):
        spread = jnp.broadcast_to(trace_ref[source : source + 1], (LAGS, width))
        shifted = pltpu.roll(spread, 0, 1, stride=1, stride_axis=0)
        out_ref[source * LAGS : (source + 1) * LAGS] = shifted.astype(jnp.bfloat16)


def hankel(traces):
    sources, samples = traces.shape
    width = samples + 128
    padded = jnp.pad(traces.astype(jnp.float32), ((0, 0), (0, 128)))
    return pl.pallas_call(
        hankel_kernel,
        out_shape=jax.ShapeDtypeStruct((sources * LAGS, width), jnp.bfloat16),
        grid=(sources // 8,),
        in_specs=[pl.BlockSpec((8, width), lambda i: (i, 0))],
        out_specs=pl.BlockSpec((8 * LAGS, width), lambda i: (i, 0)),
        compiler_params=params(),
        cost_estimate=pl.CostEstimate(
            flops=sources * LAGS * width, bytes_accessed=2 * sources * LAGS * width, transcendentals=0
        ),
        name="hankel",
    )(padded)


def at_end(spot):
    return (spot == 0) | (spot == 3)


def origin(slot, me):
    spot, side = me >> 1, me & 1
    near = spot < 2
    there = [
        spot,
        spot ^ 1,
        jnp.where(near, 2, 1),
        jnp.where(near, 3, 0),
    ][slot]
    return 2 * there + side


def correlate_kernel(rows, two, aliased, scale, me_ref, *refs):
    refs = list(refs)
    hankels = [refs.pop(0) for _ in range(rows)]
    first = refs.pop(0)
    second = refs.pop(0) if two else None
    if aliased:
        refs.pop(0)
    held = refs.pop()
    out_ref = refs.pop(0)
    depth, width = first.shape
    step = pl.program_id(0)
    each = hankels[0].shape[0] // ROWS

    @pl.when(step == 0)
    def _():
        held[depth:] = jnp.zeros((held.shape[0] - depth, width), held.dtype)
        if two:
            end = at_end(me_ref[0] >> 1)

            @pl.when(end)
            def _():
                pltpu.sync_copy(first, held.at[pl.ds(0, depth)])

            @pl.when(jnp.logical_not(end))
            def _():
                pltpu.sync_copy(second, held.at[pl.ds(0, depth)])
        else:
            pltpu.sync_copy(first, held.at[pl.ds(0, depth)])

    def product(ref, at):
        lagged = ref[pl.ds(pl.multiple_of(at * ROWS, ROWS), ROWS), :]
        return jnp.dot(lagged, held[...], preferred_element_type=jnp.float32) * scale

    if rows == 1:
        out_ref[...] = product(hankels[0], step).reshape(out_ref.shape).astype(out_ref.dtype)
        return
    sent_ref = refs.pop(0)

    @pl.when(step < each)
    def _():
        sent_ref[...] = product(hankels[1], step).reshape(sent_ref.shape).astype(sent_ref.dtype)

    @pl.when(step >= each)
    def _():
        out_ref[...] = product(hankels[0], step - each).reshape(out_ref.shape)


def correlate(hankels, operands, me, place, scale, out, channels, sent=False):
    lanes, span = hankels[0].shape
    sources = lanes // LAGS
    depth, width = operands[0].shape
    group = ROWS // LAGS
    each = lanes // ROWS
    rows = len(hankels)
    skip = (rows - 1) * each
    resident = pl.BlockSpec(memory_space=pltpu.VMEM)
    in_specs = [resident] * rows
    in_specs += [pl.BlockSpec(memory_space=pl.ANY)] * len(operands)
    arguments = [*hankels, *operands]
    aliases = {}
    if out is not None and not sent:
        in_specs.append(pl.BlockSpec(memory_space=pl.ANY))
        arguments.append(out)
        aliases = {len(arguments): 0}
    sent_shape = jax.ShapeDtypeStruct((sources, LAGS, width), jnp.bfloat16)
    sent_spec = pl.BlockSpec((group, LAGS, width), lambda i, me: (jnp.minimum(i, each - 1), 0, 0))
    out_shape = [jax.ShapeDtypeStruct((1, sources, LAGS, channels), jnp.float32)]
    out_specs = [
        pl.BlockSpec(
            (pl.Element(1), pl.Element(group), pl.Element(LAGS), pl.Element(width)),
            lambda i, me: (
                0,
                jnp.maximum(i - skip, 0) * group,
                0,
                pl.multiple_of(place(me[0]), 128),
            ),
        )
    ]
    if rows == 2:
        out_shape.append(sent_shape)
        out_specs.append(sent_spec)
    if sent:
        out_shape, out_specs = [sent_shape], [sent_spec]
    return pl.pallas_call(
        functools.partial(correlate_kernel, rows, len(operands) == 2, bool(aliases), scale),
        out_shape=out_shape,
        grid_spec=pltpu.PrefetchScalarGridSpec(
            num_scalar_prefetch=1,
            grid=(rows * each,),
            in_specs=in_specs,
            out_specs=out_specs,
            scratch_shapes=[pltpu.VMEM((span, width), jnp.bfloat16)],
        ),
        input_output_aliases=aliases,
        compiler_params=params(),
        cost_estimate=pl.CostEstimate(
            flops=2 * rows * lanes * span * width,
            bytes_accessed=2 * depth * width + 4 * lanes * width,
            transcendentals=0,
        ),
        name="correlate",
    )(me, *arguments)


def store_kernel(me_ref, got_ref, kept_ref, out_ref):
    out_ref[...] = got_ref[...].astype(jnp.float32)[None]


def store(got, me, place, out):
    sources, lags, width = got.shape
    group = ROWS // LAGS
    return pl.pallas_call(
        store_kernel,
        out_shape=jax.ShapeDtypeStruct(out.shape, out.dtype),
        grid_spec=pltpu.PrefetchScalarGridSpec(
            num_scalar_prefetch=1,
            grid=(sources // group,),
            in_specs=[
                pl.BlockSpec((group, lags, width), lambda i, me: (i, 0, 0)),
                pl.BlockSpec(memory_space=pl.ANY),
            ],
            out_specs=pl.BlockSpec(
                (pl.Element(1), pl.Element(group), pl.Element(lags), pl.Element(width)),
                lambda i, me: (0, i * group, 0, pl.multiple_of(place(me[0]), 128)),
            ),
        ),
        input_output_aliases={2: 0},
        compiler_params=params(),
        cost_estimate=pl.CostEstimate(
            flops=0, bytes_accessed=6 * sources * lags * width, transcendentals=0
        ),
        name="store",
    )(me, got, out)


def hop(array, pairs):
    return lax.ppermute(array, "src", pairs)


def line_of_four(strain, dead_mask, src_index):
    samples, channels = strain.shape
    devices = lax.axis_size("src")
    line = devices // 2
    count = len(WIDTHS)
    offsets = [sum(WIDTHS[:c]) for c in range(count)]
    total = channels * devices
    own = src_index.shape[0] // devices
    scale = 1.0 / math.sqrt(samples)
    me = lax.axis_index("src")

    def along(pairs):
        return [(2 * a + s, 2 * b + s) for a, b in pairs for s in range(2)]

    outer = along([(0, 1), (1, 0), (2, 3), (3, 2)])
    inner = along([(1, 2), (2, 1)])
    outward = along([(1, 0), (2, 3)])
    across = [(i, i ^ 1) for i in range(devices)]

    def masked(rows):
        return jnp.where(dead_mask > 0, rows, jnp.zeros((), rows.dtype))

    def around(rows):
        trail = passed_along(rows(0, SPAN), "win", -1)
        lead = passed_along(rows(samples - HALF, samples), "win", 1)
        return lead, trail

    raw = mask_first(strain, dead_mask, WIDTHS[0])
    raw_out = hop(raw, outer)
    raw_in = hop(raw, inner)
    lead, trail = around(lambda a, b: masked(strain[a:b]))
    alive = (dead_mask > 0).astype(jnp.int32)
    flats = normalize_chunks(strain, alive, lead, trail, WIDTHS)

    here = jnp.reshape(me, (1,)).astype(jnp.int32)
    theirs, mine = select_sources(flats, src_index, here, samples, own)
    heard = hop(theirs, across)
    blocks = [
        mine[by * own : (by + 1) * own] + heard[by * own : (by + 1) * own] for by in range(line)
    ]
    traces = blocks[0]
    for by in range(1, line):
        traces = traces + hop(blocks[by], along([(i, (i + by) % line) for i in range(line)]))
    partner_traces = hop(traces, across)
    own_rows = hankel(traces)
    partner_rows = hankel(partner_traces)

    def hops(arrays, pairs):
        return [hop(a, pairs) for a in arrays]

    def received(chunk):
        before, after = around(lambda a, b: chunk[a:b])
        (flat,) = normalize_chunks(chunk, None, before, after, WIDTHS[:1])
        return flat

    first_out = [received(raw_out)]
    first_in = [received(raw_in)]
    first_out += [hop(flats[c], outer) for c in range(1, count)]
    first_in += [hop(flats[c], inner) for c in range(1, count)]
    swapped = hop(flats[SHARED], across)
    second_out = hops(first_in, outward)
    second_in = hops(first_out, inner)
    third_out = hops(second_in, outward)

    arrivals = [
        [[f] for f in flats],
        [[f] for f in first_out],
        [list(pair) for pair in zip(second_out, first_in)],
        [list(pair) for pair in zip(third_out, second_in)],
    ]
    out = None
    waiting = []

    def place(slot, c, partner):
        return lambda me: (origin(slot, me) ^ partner) * channels + offsets[c]

    def add(slot, c, partner, chunk, hankels):
        nonlocal out
        out, *sent = correlate(
            hankels, chunk, here, place(slot, c, partner), scale, out, total
        )
        return sent

    def keep():
        nonlocal out
        out = store(*waiting.pop(0), out)

    add(0, SHARED, 0, [flats[SHARED]], [own_rows])
    for slot, c in STEPS:
        chunk = arrivals[slot][c]
        if slot < line - 1:
            (made,) = add(slot, c, 0, chunk, [own_rows, partner_rows])
        else:
            (made,) = correlate(
                [partner_rows], chunk, here, place(slot, c, 0), scale, out, total, sent=True
            )
            add(slot, c, 0, chunk, [own_rows])
        waiting.append((hop(made, across), here, place(slot, c, 1)))
        if (slot, c) == (0, count - 1):
            add(0, SHARED, 1, [swapped], [own_rows])
        for _ in range(STORED.get((slot, c), 0)):
            keep()
    while waiting:
        keep()
    return out


def gathered(strain, dead_mask, src_index):
    samples, channels = strain.shape
    devices = lax.axis_size("src")
    scale = 1.0 / math.sqrt(samples)
    masked = jnp.where(dead_mask > 0, strain, jnp.zeros((), strain.dtype))
    lead = passed_along(masked[samples - HALF :], "win", 1)
    trail = passed_along(masked[:SPAN], "win", -1)
    rows = jnp.concatenate([lead, masked, trail], axis=0).astype(jnp.float32)
    sums = lax.reduce_window(
        jnp.abs(rows), jnp.zeros((), jnp.float32), lax.add, (2 * HALF + 1, 1), (1, 1), "VALID"
    )
    center = rows[HALF : rows.shape[0] - HALF]
    flat = (center / (sums / (2 * HALF + 1) + EPSILON)).astype(jnp.bfloat16)
    offset = lax.axis_index("src") * channels
    onehot = (src_index[:, None] - offset == jnp.arange(channels, dtype=jnp.int32)[None, :]).astype(
        jnp.bfloat16
    )
    selected = lax.dot_general(
        onehot, flat[:samples], (((1,), (1,)), ((), ())), preferred_element_type=jnp.float32
    )
    traces = lax.psum_scatter(
        selected.astype(jnp.bfloat16), "src", scatter_dimension=0, tiled=True
    )
    sources = traces.shape[0]
    tail = flat.shape[0] - samples
    shifted = [jnp.pad(traces, ((0, 0), (lag, tail - lag))) for lag in range(LAGS)]
    lagged = jnp.stack(shifted, axis=1).reshape(sources * LAGS, flat.shape[0])
    everywhere = lax.all_gather(flat, "src", axis=1, tiled=True)
    joined = jnp.dot(lagged, everywhere, preferred_element_type=jnp.float32) * scale
    return joined.reshape(1, sources, LAGS, channels * devices)


def lined(devices, channels):
    return devices == 8 and channels == sum(WIDTHS)


def shards(strain, dead_mask, src_index):
    if lined(lax.axis_size("src"), strain.shape[1]):
        return line_of_four(strain, dead_mask, src_index)
    return gathered(strain, dead_mask, src_index)


def solution(mesh):
    in_specs = (P("win", "src"), P("win", "src"), P())
    out_specs = P("win", "src", None, None)
    return jax.shard_map(shards, mesh=mesh, in_specs=in_specs, out_specs=out_specs, check_vma=False)
```
